32 devices in a mesh: row: 8 (over y, x, core), col: 4 (over z).
Axes of the slice: x: 2, y: 2, z: 4, core: 2. Of those that a mesh axis runs over, the one named last changes fastest.
Arguments:
- start_vectors: bfloat16 [16384, 128], P(('row', 'col')), may hold values from -6 to 6
- tiles: bfloat16 [8, 128, 128, 128], P('row', 'col'), may hold values from -0.09375 to 0.09375
- tile_rows: int32 [8, 128], P('row', 'col'), may hold values from 0 to 15, as said below
- tile_cols: int32 [8, 128], P('row', 'col'), may hold values from 0 to 19
- tile_counts: int32 [8, 4], P('row', 'col'), may hold values from 4 to 32, as said below
- center: float32 [1], replicated, may hold values from -1 to 1
- half_width: float32 [1], replicated, may hold values from 2 to 3
Outputs:
- filtered: bfloat16 [16384, 128], P(('row', 'col'))
The draws below stay inside these ranges and needn't reach their ends.
Inputs may be any that keep to these rules, and one draw needn't show every extreme that they name: On each device the 32 slots name different places (tile_rows, tile_cols); only the first tile_counts slots are in use. `tile_counts`: some device uses exactly 32 slots.
All inputs are finite; a program needn't handle non-finite values.
Results may differ from the reference program's by a relative error of at most 0.009.
Values may be sent and summed in bfloat16 or wider, within the bound.
A program may use at most 64 MiB of HBM per device.

```python
import jax
import jax.numpy as jnp
from jax import lax

SEG = 2048
TILE = 128
NV = 128
MAXT = 32
NSEG = 8
PIECES = 4
BLOCKS = 5
TROWS = 16
TCOLS = 4
STATES = 16384
SLOTS = 128


def tile_layout(key):
    base_key = jax.random.fold_in(key, 7321)
    key_list = jax.random.split(base_key, NSEG * PIECES)

    def one_device(device_key):
        return jax.random.permutation(device_key, TROWS * BLOCKS * TCOLS)[:MAXT]
    places = jax.vmap(one_device)(key_list)
    return places.reshape(NSEG, PIECES * MAXT).astype(jnp.int32)


def draw_tile_rows(key, part):
    return (tile_layout(key) // (BLOCKS * TCOLS)).astype(jnp.int32)


def draw_tile_cols(key, part):
    return (tile_layout(key) % (BLOCKS * TCOLS)).astype(jnp.int32)


def draw_tile_counts(key, part):
    base_key = jax.random.fold_in(key, 9157)
    level_key, full_key = jax.random.split(base_key)
    lowest = max(MAXT // 8, 1)
    level_draw = jax.random.randint(level_key, (NSEG * PIECES,), 0, 64)
    counts = lowest + (MAXT - lowest) * level_draw * level_draw // 3969
    fullest = jax.random.randint(full_key, (), 0, NSEG * PIECES)
    counts = jnp.where(jnp.arange(NSEG * PIECES) == fullest, MAXT, counts)
    return counts.reshape(NSEG, PIECES).astype(jnp.int32)


def block_levels(own_key, dims, pieces, least, high):
    gain, own = 1.0, jax.random.fold_in(own_key, 6)
    for dim, parts in pieces:
        heights = jnp.exp(jax.random.uniform(jax.random.fold_in(own, dim), (parts,), jnp.float32, least / len(pieces), high / len(pieces)))
        gain = gain * jnp.repeat(heights, dims[dim] // parts).reshape([-1 if axis == dim else 1 for axis in range(len(dims))])
    return gain


def bell_draw(stream_key, shape, scale, bound, cuts=(), kind=jnp.bfloat16):
    values = scale * jax.random.normal(stream_key, shape, jnp.float32)
    if cuts:
        values = values * block_levels(stream_key, shape, cuts, -0.22, 0.18)
    return jnp.clip(values, -bound, bound).astype(kind)


def setup_inputs(seed: int = 0) -> dict:
    streams_of = jax.random.split(jax.random.key(seed), 8)
    return {
        "start_vectors": bell_draw(streams_of[0], (STATES, NV), 1.0, 6.0, ((0, 32),)),
        "tiles": bell_draw(streams_of[1], (NSEG, SLOTS, TILE, TILE), (MAXT * TILE) ** -0.5, 0.09375, ((0, 8), (1, 4))),
        "tile_rows": draw_tile_rows(jax.random.fold_in(streams_of[7], 71), 0),
        "tile_cols": draw_tile_cols(jax.random.fold_in(streams_of[7], 71), 0),
        "tile_counts": draw_tile_counts(jax.random.fold_in(streams_of[7], 71), 0),
        "center": jnp.clip(jax.random.uniform(streams_of[5], (1,), jnp.float32, -1.0, 1.0), -1.0, 1.0),
        "half_width": jnp.clip(jax.random.uniform(streams_of[6], (1,), jnp.float32, 2.0, 3.0), 2.0, 3.0),
    }


def apply_operator(vectors, tiles, tile_rows, tile_cols, tile_counts):
    segments = vectors.reshape(NSEG, TROWS, TILE, NV)
    zero_index = jnp.zeros((), jnp.int32)

    def one_device(totals, device_index):
        direct_sum, back_sum = totals
        seg_row = (device_index // PIECES).astype(jnp.int32)
        piece_index = (device_index % PIECES).astype(jnp.int32)
        slot_start = (piece_index * MAXT).astype(jnp.int32)
        tile_block = lax.dynamic_slice(tiles, (seg_row, slot_start, zero_index, zero_index), (1, MAXT, TILE, TILE))[0]
        rows_list = lax.dynamic_slice(tile_rows, (seg_row, slot_start), (1, MAXT))[0]
        cols_list = lax.dynamic_slice(tile_cols, (seg_row, slot_start), (1, MAXT))[0]
        live_count = lax.dynamic_slice(tile_counts, (seg_row, piece_index), (1, 1))[0, 0]
        in_use = (jnp.arange(MAXT, dtype=jnp.int32) < live_count).astype(jnp.float32)
        seg_col = ((seg_row + cols_list // TCOLS) % NSEG).astype(jnp.int32)
        tile_col = (piece_index * TCOLS + cols_list % TCOLS).astype(jnp.int32)
        tile_float = tile_block.astype(jnp.float32)
        inputs = segments[seg_col, tile_col].astype(jnp.float32)
        forward = jnp.einsum("tab,tbn->tan", tile_float, inputs, precision=lax.Precision.HIGHEST) * in_use[:, None, None]
        direct_sum = direct_sum.at[seg_row, rows_list].add(forward)
        own_rows = segments[seg_row, rows_list].astype(jnp.float32)
        backward = jnp.einsum("tab,tan->tbn", tile_float, own_rows, precision=lax.Precision.HIGHEST) * in_use[:, None, None]
        back_sum = back_sum.at[seg_col, tile_col].add(backward)
        return (direct_sum, back_sum), None

    empty_sum = jnp.zeros((NSEG, TROWS, TILE, NV), jnp.float32)
    totals, unused = lax.scan(one_device, (empty_sum, empty_sum), jnp.arange(NSEG * PIECES, dtype=jnp.int32))
    return (totals[0] + totals[1]).reshape(NSEG * SEG, NV)


def reference(start_vectors, tiles, tile_rows, tile_cols, tile_counts, center, half_width):
    shift_value = center[0]
    width_value = half_width[0]
    start_float = start_vectors.astype(jnp.float32)
    applied = apply_operator(start_vectors, tiles, tile_rows, tile_cols, tile_counts)
    first_step = ((applied - shift_value * start_float) / width_value).astype(jnp.bfloat16)
    applied = apply_operator(first_step, tiles, tile_rows, tile_cols, tile_counts)
    filtered = 2.0 * (applied - shift_value * first_step.astype(jnp.float32)) / width_value - start_float
    return filtered.astype(jnp.bfloat16)
```

```python
import functools

import jax
import jax.numpy as jnp
from jax import lax
from jax.experimental import pallas as pl
from jax.experimental.pallas import tpu as pltpu
from jax.sharding import PartitionSpec as P

CHUNKS = 2
UNROLL = 16
MESH_ID = pl.DeviceIdType.MESH
GATHER_TREES = (("tail", "tail"), ("tail", "tail"))
REDUCE_TREES = (("tail", "tail"), ("tail", "tail"))
ORDER = ()


def parent(kind, length, dist):
    if kind == "chain":
        return dist - 1
    if kind == "tail":
        return dist - 1 if dist == length and length >= 2 else 0
    if kind == "tail3":
        return dist - 1 if dist == length and length >= 3 else 0
    return 0


def side(c, sgn, C):
    return c if sgn > 0 else C - 1 - c


def default_order(K, C):
    far = range(2, C - 1)
    order = [("Gs", 0, h) for h in range(K)]
    for t in range(2):
        for h in range(K):
            order += [("XF", t, h), ("GF1", t, h), ("D", t, h)]
        for h in range(K):
            order += [("GF%d" % d, t, h) for d in far]
            order += [("RM%d" % d, t, h) for d in reversed(far)] + [("RM1", t, h)]
            order += [("B", t, h), ("RX", t, h)]
        for h in range(K):
            order.append(("E", t, h))
            if t == 0:
                order.append(("Gs", 1, h))
    return order


def full_order(K, C, hq):
    base = [(s[:-2], int(s[-2]), int(s[-1])) for s in ORDER] or default_order(K, C)
    known = set(base)
    order = []
    for name, t, h in base:
        if name == "B":
            order += [("GF%d" % d, t, h) for d in range(1, C - 1) if ("GF%d" % d, t, h) not in known]
        if name == "E":
            order += [("RM%d" % d, t, h) for d in range(C - 2, 0, -1) if ("RM%d" % d, t, h) not in known]
        if name == "XF":
            order += [("XF%d" % d, t, h) for d in range(1, hq + 1)]
        elif name == "RX":
            order += [("RX%d" % d, t, h) for d in range(hq, 0, -1)]
        else:
            if name == "D":
                order += [("XF%d" % d, t, h) for d in range(1, hq + 1)
                          if ("XF%d" % d, t, h) not in known and ("XF", t, h) not in known]
            if name == "E":
                order += [("RX%d" % d, t, h) for d in range(hq, 0, -1)
                          if ("RX%d" % d, t, h) not in known and ("RX", t, h) not in known]
            order.append((name, t, h))
    return order


def filter_kernel(
    dims, x_ref, tiles_ref, rows_ref, cols_ref, counts_ref, center_ref, width_ref, out_ref, *scratch,
):
    R, C, half, pt, slots, vec, size = dims
    K = CHUNKS
    vc = vec // K
    hq = half // 2
    ways = 2 * (C - 1)
    it = iter(scratch)

    def pair():
        return [[next(it) for _ in range(K)] for _ in range(2)]

    win, seg, pair_out, row_out, pair_in, row_in = pair(), pair(), pair(), pair(), pair(), pair()
    col_out, col_fin, col_mid = pair(), pair(), pair()
    back = [next(it) for _ in range(K)]
    direct = [next(it) for _ in range(K)]
    x_in, result, tiles, keys, table = next(it), next(it), next(it), next(it), next(it)
    row_of, col_of, links = next(it), next(it), next(it)
    local, row_send, row_recv, col_send, col_recv = next(it), next(it), next(it), next(it), next(it)

    r = lax.axis_index("row")
    c = lax.axis_index("col")
    k = lax.rem(r, 2)
    partner = r + 1 - 2 * k

    def among(test):
        members = [n for n in range(C) if test(n)]
        if len(members) in (0, C):
            return bool(members)
        cond = None
        for lo in members:
            if lo - 1 in members:
                continue
            hi = lo
            while hi + 1 in members:
                hi += 1
            one = c == lo if lo == hi else c <= hi if lo == 0 else c >= lo if hi == C - 1 else (c >= lo) & (c <= hi)
            cond = one if cond is None else cond | one
        return cond

    def when(cond, act):
        if cond is True:
            act()
        elif cond is not False:
            pl.when(cond)(act)

    barrier = pltpu.get_barrier_semaphore()
    row_peers = sorted({d % R for d in range(2, half + 1, 2)} | {-d % R for d in range(2, half + 1, 2)})
    for off in row_peers:
        pl.semaphore_signal(barrier, inc=1, device_id={"row": lax.rem(r + off, R)}, device_id_type=MESH_ID)
    pl.semaphore_signal(barrier, inc=1, device_id={"row": partner}, device_id_type=MESH_ID)
    for off in range(1, C):
        pl.semaphore_signal(barrier, inc=1, device_id={"col": lax.rem(c + off, C)}, device_id_type=MESH_ID)

    load_x = pltpu.make_async_copy(x_ref, x_in, local.at[0])
    load_x.start()
    smem_loads = [
        pltpu.make_async_copy(rows_ref, row_of, local.at[1]),
        pltpu.make_async_copy(cols_ref, col_of, local.at[2]),
    ]
    key_loads = [
        pltpu.make_async_copy(rows_ref, keys.at[0], local.at[3]),
        pltpu.make_async_copy(cols_ref, keys.at[1], local.at[4]),
    ]
    for copy in key_loads + smem_loads:
        copy.start()
    fetch = pltpu.make_async_copy(tiles_ref.at[0], tiles, local.at[5])
    fetch.start()

    def way(sgn, d):
        return 2 * (d - 1) + (0 if sgn > 0 else 1)

    def tiles_at(ref, slot):
        return ref.at[pl.ds(slot * pt, pt)]

    sgns = (1, -1)
    dists = range(1, C)
    final = {}
    for t in range(2):
        for h in range(K):
            for sgn in sgns:
                for d in dists:
                    def test(n, t=t, h=h, sgn=sgn, d=d):
                        return d <= side(n, sgn, C) and parent(REDUCE_TREES[t][h], side(n, sgn, C), d) == 0
                    cond = among(test)
                    final[t, h, sgn, d] = cond
                    if cond is not True and cond is not False:
                        def clear(t=t, h=h, sgn=sgn, d=d):
                            tiles_at(col_fin[t][h], way(sgn, d))[...] = jnp.zeros((pt, vc, size), jnp.bfloat16)
                        pl.when(jnp.logical_not(cond))(clear)
            tiles_at(pair_in[t][h], hq)[...] = jnp.zeros((pt, vc, size), jnp.bfloat16)
    for h in range(K):
        back[h][slots] = jnp.zeros((vc, size), jnp.float32)
        direct[h][slots] = jnp.zeros((vc, size), jnp.float32)

    load_x.wait()
    for j in range(pt):
        block = x_in[j * size:(j + 1) * size, :].astype(jnp.float32).T.astype(jnp.bfloat16)
        for h in range(K):
            part = block[h * vc:(h + 1) * vc, :]
            win[0][h][j] = part
            seg[0][h][c * pt + j] = part
    pl.semaphore_wait(barrier, len(row_peers) + 1 + C - 1)

    drains = []

    def start(copy, cond=True):
        when(cond, copy.start)
        drains.append((copy, cond))

    def to_row(src, dst, t, h, send, recv, row):
        return pltpu.make_async_remote_copy(
            src_ref=src, dst_ref=dst, send_sem=row_send.at[t, h, send], recv_sem=row_recv.at[t, h, recv],
            device_id={"row": row}, device_id_type=MESH_ID)

    def to_col(src, dst, t, h, send, recv, col):
        return pltpu.make_async_remote_copy(
            src_ref=src, dst_ref=dst, send_sem=col_send.at[t, h, send], recv_sem=col_recv.at[t, h, recv],
            device_id={"col": col}, device_id_type=MESH_ID)

    def up(d):
        return lax.rem(r + d, R)

    def piece_copy(t, h, d):
        return to_row(tiles_at(win[t][h], 0), tiles_at(win[t][h], 2 * d), t, h, 2 * d, 2 * d, up(R - 2 * d))

    def partner_copy(t, h, d):
        slot = 2 * d - 1 + 2 * k
        return to_row(tiles_at(win[t][h], 2 * d), tiles_at(win[t][h], slot), t, h, slot, slot, partner)

    def piece_arrival(t, h, b):
        view = tiles_at(win[t][h], b)
        return to_row(view, view, t, h, b, b, partner)

    def pair_copy(t, h, j):
        at = half + j
        return to_row(
            tiles_at(pair_out[t][h], j - 1), tiles_at(pair_in[t][h], j - 1), t, h, at, at, partner)

    def row_copy(t, h, d):
        at = half + hq + d
        return to_row(
            tiles_at(row_out[t][h], d - 1), tiles_at(row_in[t][h], d - 1), t, h, at, at, up(2 * d))

    def col_piece(t, h, sgn, d, hop):
        p = c - sgn * d
        view = tiles_at(seg[t][h], p)
        src = view if d else tiles_at(win[t][h], 0)
        send = way(sgn, hop) if d == 0 else ways + way(sgn, d)
        return to_col(src, view, t, h, send, p, c + sgn * hop)

    def col_arrival(t, h, sgn, d):
        p = c - sgn * d
        view = tiles_at(seg[t][h], p)
        return to_col(view, view, t, h, 0, p, p)

    def gather_child(t, h, sgn, d, hop):
        kind = GATHER_TREES[t][h]

        def test(n):
            root = n - sgn * d
            if not 0 <= root < C or not 0 <= n + sgn * hop < C:
                return False
            length = side(C - 1 - root, sgn, C)
            return parent(kind, length, d + hop) == d
        return among(test)

    def start_gather(t, h):
        for d in range(hq, 0, -1):
            start(piece_copy(t, h, d))
        start(partner_copy(t, h, 0), k == 1)
        for hop in reversed(dists):
            for sgn in sgns:
                cond = gather_child(t, h, sgn, 0, hop)
                if cond is not False:
                    start(col_piece(t, h, sgn, 0, hop), cond)

    def forward_row(t, h, d):
        piece_arrival(t, h, 2 * d).wait_recv()
        start(partner_copy(t, h, d), True if d < hq else k == 0)

    def forward_col(t, h, d):
        for sgn in sgns:
            cond = gather_child(t, h, sgn, d, 1)
            if cond is False:
                continue
            when(cond, col_arrival(t, h, sgn, d).wait_recv)
            start(col_piece(t, h, sgn, d, 1), cond)

    def products(source, index_ref, side_row, sums, transposed):
        contract = (((1,), (0,)), ((), ())) if transposed else (((1,), (1,)), ((), ()))

        def one(s, carry):
            term = lax.dot_general(
                source[index_ref[0, s]], tiles[s], contract,
                preferred_element_type=jnp.float32)
            sums[s] = sums[links[side_row, s]] + term
            return carry

        lax.fori_loop(0, slots, one, 0, unroll=UNROLL)

    def reduce_groups(t, h, sgn, d):
        kind = REDUCE_TREES[t][h]

        def of(n):
            dest = n + sgn * d
            if not 0 <= dest < C:
                return None
            length = side(dest, sgn, C)
            return parent(kind, length, d), d < length and parent(kind, length, d + 1) == d
        found = sorted({of(n) for n in range(C)} - {None})
        return [(left, helped, among(lambda n: of(n) == (left, helped))) for left, helped in found]

    def reduce_copy(t, h, sgn, d, left):
        w = way(sgn, d)
        src = tiles_at(col_out[t][h], w)
        if left == 0:
            return to_col(src, tiles_at(col_fin[t][h], w), t, h, 2 * ways + w, C + w, c + sgn * d)
        m = way(sgn, left)
        return to_col(src, tiles_at(col_mid[t][h], m), t, h, 2 * ways + w, C + ways + m, c + sgn * (d - left))

    def mid_arrival(t, h, sgn, d):
        m = way(sgn, d)
        view = tiles_at(col_mid[t][h], m)
        return to_col(view, view, t, h, 0, C + ways + m, c)

    def fin_arrival(t, h, sgn, d):
        w = way(sgn, d)
        view = tiles_at(col_fin[t][h], w)
        return to_col(view, view, t, h, 0, C + w, c)

    def pass_on(t, h, d, want):
        for sgn in sgns:
            for left, helped, cond in reduce_groups(t, h, sgn, d):
                if helped != want:
                    continue

                def act(sgn=sgn, helped=helped):
                    if helped:
                        mid_arrival(t, h, sgn, d).wait_recv()
                    dest = c + sgn * d
                    for j in range(pt):
                        value = direct[h][links[2, dest * pt + j]]
                        if helped:
                            value += col_mid[t][h][way(sgn, d) * pt + j].astype(jnp.float32)
                        col_out[t][h][way(sgn, d) * pt + j] = value.astype(jnp.bfloat16)
                when(cond, act)
                start(reduce_copy(t, h, sgn, d, left), cond)

    def do_direct(t, h):
        for b in range(1, half + 1, 2):
            piece_arrival(t, h, b).wait_recv()
        products(win[t][h], col_of, 0, direct[h], False)
        for d in reversed(dists):
            pass_on(t, h, d, False)

    def do_back(t, h):
        for sgn in sgns:
            for d in dists:
                def test(n, sgn=sgn, d=d):
                    return d <= side(n, sgn, C)

                def sent(n, sgn=sgn, d=d):
                    root, nxt = n - sgn * d, n + sgn
                    return 0 <= nxt < C and parent(GATHER_TREES[t][h], side(C - 1 - root, sgn, C), d + 1) == d
                cond = among(lambda n: test(n) and not sent(n))
                if cond is not False:
                    when(cond, col_arrival(t, h, sgn, d).wait_recv)
        products(seg[t][h], row_of, 1, back[h], True)
        for i in range(1, hq + 1):
            for j in range(pt):
                pair_out[t][h][(i - 1) * pt + j] = back[h][links[3, (2 * i - 1) * pt + j]].astype(jnp.bfloat16)
            start(pair_copy(t, h, i))

    def return_row(t, h, d):
        arrival = pair_copy(t, h, d)
        if d < hq:
            slot = d - 1 + k
            view = tiles_at(pair_in[t][h], slot)
            to_row(view, view, t, h, half + 1 + slot, half + 1 + slot, partner).wait_recv()
        else:
            slot = d - 1 + k
            pl.when(k == 0)(arrival.wait_recv)
        for j in range(pt):
            value = back[h][links[3, 2 * d * pt + j]] + pair_in[t][h][slot * pt + j].astype(jnp.float32)
            row_out[t][h][(d - 1) * pt + j] = value.astype(jnp.bfloat16)
        start(row_copy(t, h, d))

    shift = center_ref[0]
    width = width_ref[0]

    def finish(t, h):
        pl.when(k == 1)(pair_copy(t, h, 1).wait_recv)
        for d in range(1, hq + 1):
            row_copy(t, h, d).wait_recv()
        for sgn in sgns:
            for d in dists:
                cond = final[t, h, sgn, d]
                if cond is not False:
                    when(cond, fin_arrival(t, h, sgn, d).wait_recv)
        slot = jnp.where(k == 1, 0, hq)
        for j in range(pt):
            total = back[h][links[3, j]] + direct[h][links[2, c * pt + j]]
            total += pair_in[t][h][slot * pt + j].astype(jnp.float32)
            for d in range(hq):
                total += row_in[t][h][d * pt + j].astype(jnp.float32)
            for sgn in sgns:
                for d in dists:
                    if final[t, h, sgn, d] is not False:
                        total += col_fin[t][h][way(sgn, d) * pt + j].astype(jnp.float32)
            begin = win[0][h][j].astype(jnp.float32)
            if t == 0:
                first = ((total - shift * begin) / width).astype(jnp.bfloat16)
                win[1][h][j] = first
                seg[1][h][c * pt + j] = first
            else:
                first = win[1][h][j].astype(jnp.float32)
                result[j, h * vc:(h + 1) * vc, :] = 2.0 * (total - shift * first) / width - begin

    def link_slots():
        for copy in key_loads:
            copy.wait()
        count = counts_ref[0, 0]
        sub = lax.broadcasted_iota(jnp.int32, (slots, slots), 0)
        lane = lax.broadcasted_iota(jnp.int32, (slots, slots), 1)
        sub_w = lax.broadcasted_iota(jnp.int32, (slots, size), 0)
        lane_w = lax.broadcasted_iota(jnp.int32, (slots, size), 1)
        for i in range(2):
            key = jnp.broadcast_to(keys[i], (slots, slots))
            column = jnp.max(jnp.where(lane == sub, key, -1), axis=1, keepdims=True)
            same = (column == key) & (sub < lane) & (sub < count)
            before = jnp.max(jnp.where(same, sub, -1), axis=0, keepdims=True)
            table[i:i + 1, 0:slots] = jnp.where(before < 0, slots, before)
            hit = (column == lane_w) & (sub_w < count)
            last = jnp.max(jnp.where(hit, sub_w, -1), axis=0, keepdims=True)
            table[2 + i:3 + i, :] = jnp.where(last < 0, slots, last)
        publish = pltpu.make_async_copy(table, links, local.at[6])
        publish.start()
        for copy in smem_loads:
            copy.wait()
        publish.wait()

    waited = False
    for name, t, h in full_order(K, C, hq):
        if name in ("D", "B") and not waited:
            fetch.wait()
            waited = True
        if name == "Gs":
            start_gather(t, h)
            if (t, h) == (0, K - 1):
                link_slots()
        elif name == "D":
            do_direct(t, h)
        elif name == "B":
            do_back(t, h)
        elif name == "E":
            finish(t, h)
        else:
            act = {"XF": forward_row, "GF": forward_col, "RX": return_row}.get(name[:2])
            if act is not None:
                act(t, h, int(name[2:]))
            else:
                pass_on(t, h, int(name[2:]), True)
    for j in range(pt):
        out_ref[j * size:(j + 1) * size, :] = result[j].T.astype(jnp.bfloat16)
    for copy, cond in drains:
        when(cond, copy.wait_send)


def per_device(start_vectors, tiles, tile_rows, tile_cols, tile_counts, center, half_width):
    R = lax.axis_size("row")
    C = lax.axis_size("col")
    half = R // 2
    hq = half // 2
    piece_rows, vec = start_vectors.shape
    size = tiles.shape[-1]
    slots = tiles.shape[1]
    pt = piece_rows // size
    vc = vec // CHUNKS
    ways = 2 * (C - 1)
    smem = pl.BlockSpec(memory_space=pltpu.SMEM)
    vmem = pl.BlockSpec(memory_space=pltpu.VMEM)
    anywhere = pl.BlockSpec(memory_space=pl.ANY)
    bf, f32, i32 = jnp.bfloat16, jnp.float32, jnp.int32

    def pair(count):
        return [pltpu.VMEM((count * pt, vc, size), bf) for _ in range(2 * CHUNKS)]

    scratch = (
        pair(half + 1) + pair(C) + pair(hq) + pair(hq) + pair(hq + 1) + pair(hq)
        + pair(ways) + pair(ways) + pair(ways)
        + [pltpu.VMEM((slots + 1, vc, size), f32) for _ in range(2 * CHUNKS)]
        + [
            pltpu.VMEM((piece_rows, vec), bf), pltpu.VMEM((pt, vec, size), f32),
            pltpu.VMEM((slots, size, size), bf),
            pltpu.VMEM((2, 1, slots), i32), pltpu.VMEM((4, size), i32),
            pltpu.SMEM((1, slots), i32), pltpu.SMEM((1, slots), i32), pltpu.SMEM((4, size), i32),
            pltpu.SemaphoreType.DMA((7,)),
        ]
        + [pltpu.SemaphoreType.DMA((2, CHUNKS, half + 2 * hq + 1))] * 2
        + [pltpu.SemaphoreType.DMA((2, CHUNKS, 3 * ways))]
        + [pltpu.SemaphoreType.DMA((2, CHUNKS, C + 2 * ways))]
    )
    return pl.pallas_call(
        functools.partial(filter_kernel, (R, C, half, pt, slots, vec, size)),
        out_shape=jax.ShapeDtypeStruct((piece_rows, vec), bf),
        in_specs=[anywhere] * 4 + [smem] * 3,
        out_specs=vmem,
        scratch_shapes=scratch,
        compiler_params=pltpu.CompilerParams(
            collective_id=0, has_side_effects=True, vmem_limit_bytes=VMEM_LIMIT),
        name="filter_steps",
    )(start_vectors, tiles, tile_rows, tile_cols, tile_counts, center, half_width)


VMEM_LIMIT = 66_800_000


def solution(mesh):
    return jax.shard_map(
        per_device,
        mesh=mesh,
        in_specs=(
            P(("row", "col"), None),
            P("row", "col", None, None),
            P("row", "col"),
            P("row", "col"),
            P("row", "col"),
            P(),
            P(),
        ),
        out_specs=P(("row", "col"), None),
        check_vma=False,
    )
```

```python
import contextlib
import functools

import jax
import jax.numpy as jnp
from jax import lax
from jax.experimental import pallas as pl
from jax.experimental.pallas import tpu as pltpu
from jax.sharding import PartitionSpec as P

CHUNKS = 2
UNROLL = 16
MESH_ID = pl.DeviceIdType.MESH
GATHER_TREES = (("tail3", "tail3"), ("tail3", "tail"))
REDUCE_TREES = (("tail", "tail"), ("tail", "tail"))
ORDER = (
    "Gs00", "GF200", "XF100", "GF100", "GF101", "Gs01", "XF200", "D00",
    "XF101", "B00", "GF201", "RX200", "RX100", "XF201", "D01", "RM100",
    "B01", "RX201", "RM200", "RM201", "RX101", "RM101", "E00", "Gs10",
    "E01", "XF110", "Gs11", "XF210", "GF210", "D10", "GF110", "GF211",
    "XF111", "B10", "XF211", "GF111", "RX110", "RM210", "D11", "RX210",
    "B11", "RM110", "RM211", "RX211", "RX111", "RM111", "E10", "E11",
)
SCOPE = contextlib.nullcontext


def parent(kind, length, dist):
    if kind == "chain":
        return dist - 1
    if kind == "tail":
        return dist - 1 if dist == length and length >= 2 else 0
    if kind == "tail3":
        return dist - 1 if dist == length and length >= 3 else 0
    return 0


def side(c, sgn, C):
    return c if sgn > 0 else C - 1 - c


def default_order(K, C):
    far = range(2, C - 1)
    order = [("Gs", 0, h) for h in range(K)]
    for t in range(2):
        for h in range(K):
            order += [("XF", t, h), ("GF1", t, h), ("D", t, h)]
        for h in range(K):
            order += [("GF%d" % d, t, h) for d in far]
            order += [("RM%d" % d, t, h) for d in reversed(far)] + [("RM1", t, h)]
            order += [("B", t, h), ("RX", t, h)]
        for h in range(K):
            order.append(("E", t, h))
            if t == 0:
                order.append(("Gs", 1, h))
    return order


def full_order(K, C, hq):
    base = [(s[:-2], int(s[-2]), int(s[-1])) for s in ORDER] or default_order(K, C)
    known = set(base)
    order = []
    for name, t, h in base:
        if name == "B":
            order += [("GF%d" % d, t, h) for d in range(1, C - 1) if ("GF%d" % d, t, h) not in known]
        if name == "E":
            order += [("RM%d" % d, t, h) for d in range(C - 2, 0, -1) if ("RM%d" % d, t, h) not in known]
        if name == "XF":
            order += [("XF%d" % d, t, h) for d in range(1, hq + 1)]
        elif name == "RX":
            order += [("RX%d" % d, t, h) for d in range(hq, 0, -1)]
        else:
            if name == "D":
                order += [("XF%d" % d, t, h) for d in range(1, hq + 1)
                          if ("XF%d" % d, t, h) not in known and ("XF", t, h) not in known]
            if name == "E":
                order += [("RX%d" % d, t, h) for d in range(hq, 0, -1)
                          if ("RX%d" % d, t, h) not in known and ("RX", t, h) not in known]
            order.append((name, t, h))
    return order


def filter_kernel(
    dims, x_ref, tiles_ref, row_of, col_of, counts_ref, center_ref, width_ref, out_ref, *scratch,
):
    R, C, half, pt, slots, vec, size = dims
    K = CHUNKS
    vc = vec // K
    hq = half // 2
    ways = 2 * (C - 1)
    it = iter(scratch)

    def pair():
        return [[next(it) for _ in range(K)] for _ in range(2)]

    win, seg, pair_out, row_out, pair_in, row_in = pair(), pair(), pair(), pair(), pair(), pair()
    col_out, col_fin, col_mid = pair(), pair(), pair()
    back = [next(it) for _ in range(K)]
    direct = [next(it) for _ in range(K)]
    x_in, result, tiles, table, links = next(it), next(it), next(it), next(it), next(it)
    local, row_send, row_recv, col_send, col_recv = next(it), next(it), next(it), next(it), next(it)

    r = lax.axis_index("row")
    c = lax.axis_index("col")
    k = lax.rem(r, 2)
    partner = r + 1 - 2 * k

    def among(test):
        members = [n for n in range(C) if test(n)]
        if len(members) in (0, C):
            return bool(members)
        cond = None
        for lo in members:
            if lo - 1 in members:
                continue
            hi = lo
            while hi + 1 in members:
                hi += 1
            one = c == lo if lo == hi else c <= hi if lo == 0 else c >= lo if hi == C - 1 else (c >= lo) & (c <= hi)
            cond = one if cond is None else cond | one
        return cond

    def when(cond, act):
        if cond is True:
            act()
        elif cond is not False:
            pl.when(cond)(act)

    barrier = pltpu.get_barrier_semaphore()
    row_peers = sorted({d % R for d in range(2, half + 1, 2)} | {-d % R for d in range(2, half + 1, 2)})
    for off in row_peers:
        pl.semaphore_signal(barrier, inc=1, device_id={"row": lax.rem(r + off, R)}, device_id_type=MESH_ID)
    pl.semaphore_signal(barrier, inc=1, device_id={"row": partner}, device_id_type=MESH_ID)
    for off in range(1, C):
        pl.semaphore_signal(barrier, inc=1, device_id={"col": lax.rem(c + off, C)}, device_id_type=MESH_ID)

    load_x = pltpu.make_async_copy(x_ref, x_in, local.at[0])
    load_x.start()
    fetch = pltpu.make_async_copy(tiles_ref.at[0], tiles, local.at[1])
    fetch.start()

    def way(sgn, d):
        return 2 * (d - 1) + (0 if sgn > 0 else 1)

    def tiles_at(ref, slot):
        return ref.at[pl.ds(slot * pt, pt)]

    sgns = (1, -1)
    dists = range(1, C)
    final = {}
    for t in range(2):
        for h in range(K):
            for sgn in sgns:
                for d in dists:
                    def test(n, t=t, h=h, sgn=sgn, d=d):
                        return d <= side(n, sgn, C) and parent(REDUCE_TREES[t][h], side(n, sgn, C), d) == 0
                    cond = among(test)
                    final[t, h, sgn, d] = cond
                    if cond is not True and cond is not False:
                        def clear(t=t, h=h, sgn=sgn, d=d):
                            tiles_at(col_fin[t][h], way(sgn, d))[...] = jnp.zeros((pt, vc, size), jnp.bfloat16)
                        pl.when(jnp.logical_not(cond))(clear)
            tiles_at(pair_in[t][h], hq)[...] = jnp.zeros((pt, vc, size), jnp.bfloat16)
    for h in range(K):
        back[h][slots] = jnp.zeros((vc, size), jnp.float32)
        direct[h][slots] = jnp.zeros((vc, size), jnp.float32)

    with SCOPE("loadx"):
        load_x.wait()
    for j in range(pt):
        block = x_in[j * size:(j + 1) * size, :].astype(jnp.float32).T.astype(jnp.bfloat16)
        for h in range(K):
            part = block[h * vc:(h + 1) * vc, :]
            win[0][h][j] = part
            seg[0][h][c * pt + j] = part
    with SCOPE("greet"):
        pl.semaphore_wait(barrier, len(row_peers) + 1 + C - 1)

    drains = []

    def start(copy, cond=True):
        when(cond, copy.start)
        drains.append((copy, cond))

    def to_row(src, dst, t, h, send, recv, row):
        return pltpu.make_async_remote_copy(
            src_ref=src, dst_ref=dst, send_sem=row_send.at[t, h, send], recv_sem=row_recv.at[t, h, recv],
            device_id={"row": row}, device_id_type=MESH_ID)

    def to_col(src, dst, t, h, send, recv, col):
        return pltpu.make_async_remote_copy(
            src_ref=src, dst_ref=dst, send_sem=col_send.at[t, h, send], recv_sem=col_recv.at[t, h, recv],
            device_id={"col": col}, device_id_type=MESH_ID)

    def up(d):
        return lax.rem(r + d, R)

    def piece_copy(t, h, d):
        return to_row(tiles_at(win[t][h], 0), tiles_at(win[t][h], 2 * d), t, h, 2 * d, 2 * d, up(R - 2 * d))

    def partner_copy(t, h, d):
        slot = 2 * d - 1 + 2 * k
        return to_row(tiles_at(win[t][h], 2 * d), tiles_at(win[t][h], slot), t, h, slot, slot, partner)

    def piece_arrival(t, h, b):
        view = tiles_at(win[t][h], b)
        return to_row(view, view, t, h, b, b, partner)

    def pair_copy(t, h, j):
        at = half + j
        return to_row(
            tiles_at(pair_out[t][h], j - 1), tiles_at(pair_in[t][h], j - 1), t, h, at, at, partner)

    def row_copy(t, h, d):
        at = half + hq + d
        return to_row(
            tiles_at(row_out[t][h], d - 1), tiles_at(row_in[t][h], d - 1), t, h, at, at, up(2 * d))

    def col_piece(t, h, sgn, d, hop):
        p = c - sgn * d
        view = tiles_at(seg[t][h], p)
        src = view if d else tiles_at(win[t][h], 0)
        send = way(sgn, hop) if d == 0 else ways + way(sgn, d)
        return to_col(src, view, t, h, send, p, c + sgn * hop)

    def col_arrival(t, h, sgn, d):
        p = c - sgn * d
        view = tiles_at(seg[t][h], p)
        return to_col(view, view, t, h, 0, p, p)

    def gather_child(t, h, sgn, d, hop):
        kind = GATHER_TREES[t][h]

        def test(n):
            root = n - sgn * d
            if not 0 <= root < C or not 0 <= n + sgn * hop < C:
                return False
            length = side(C - 1 - root, sgn, C)
            return parent(kind, length, d + hop) == d
        return among(test)

    def start_gather(t, h):
        for d in range(hq, 0, -1):
            start(piece_copy(t, h, d))
        start(partner_copy(t, h, 0), k == 1)
        for hop in reversed(dists):
            for sgn in sgns:
                cond = gather_child(t, h, sgn, 0, hop)
                if cond is not False:
                    start(col_piece(t, h, sgn, 0, hop), cond)

    def forward_row(t, h, d):
        piece_arrival(t, h, 2 * d).wait_recv()
        start(partner_copy(t, h, d), True if d < hq else k == 0)

    def forward_col(t, h, d):
        for sgn in sgns:
            cond = gather_child(t, h, sgn, d, 1)
            if cond is False:
                continue
            when(cond, col_arrival(t, h, sgn, d).wait_recv)
            start(col_piece(t, h, sgn, d, 1), cond)

    def products(source, index_ref, side_row, sums, transposed):
        contract = (((1,), (0,)), ((), ())) if transposed else (((1,), (1,)), ((), ()))

        def one(s, carry):
            term = lax.dot_general(
                source[index_ref[0, s]], tiles[s], contract,
                preferred_element_type=jnp.float32)
            sums[s] = sums[links[side_row, s]] + term
            return carry

        lax.fori_loop(0, slots, one, 0, unroll=UNROLL)

    def reduce_groups(t, h, sgn, d):
        kind = REDUCE_TREES[t][h]

        def of(n):
            dest = n + sgn * d
            if not 0 <= dest < C:
                return None
            length = side(dest, sgn, C)
            return parent(kind, length, d), d < length and parent(kind, length, d + 1) == d
        found = sorted({of(n) for n in range(C)} - {None})
        return [(left, helped, among(lambda n: of(n) == (left, helped))) for left, helped in found]

    def reduce_copy(t, h, sgn, d, left):
        w = way(sgn, d)
        src = tiles_at(col_out[t][h], w)
        if left == 0:
            return to_col(src, tiles_at(col_fin[t][h], w), t, h, 2 * ways + w, C + w, c + sgn * d)
        m = way(sgn, left)
        return to_col(src, tiles_at(col_mid[t][h], m), t, h, 2 * ways + w, C + ways + m, c + sgn * (d - left))

    def mid_arrival(t, h, sgn, d):
        m = way(sgn, d)
        view = tiles_at(col_mid[t][h], m)
        return to_col(view, view, t, h, 0, C + ways + m, c)

    def fin_arrival(t, h, sgn, d):
        w = way(sgn, d)
        view = tiles_at(col_fin[t][h], w)
        return to_col(view, view, t, h, 0, C + w, c)

    def pass_on(t, h, d, want):
        for sgn in sgns:
            for left, helped, cond in reduce_groups(t, h, sgn, d):
                if helped != want:
                    continue

                def act(sgn=sgn, helped=helped):
                    if helped:
                        mid_arrival(t, h, sgn, d).wait_recv()
                    dest = c + sgn * d
                    for j in range(pt):
                        value = direct[h][links[2, dest * pt + j]]
                        if helped:
                            value += col_mid[t][h][way(sgn, d) * pt + j].astype(jnp.float32)
                        col_out[t][h][way(sgn, d) * pt + j] = value.astype(jnp.bfloat16)
                when(cond, act)
                start(reduce_copy(t, h, sgn, d, left), cond)

    def do_direct(t, h):
        for b in range(1, half + 1, 2):
            piece_arrival(t, h, b).wait_recv()
        products(win[t][h], col_of, 0, direct[h], False)
        for d in reversed(dists):
            pass_on(t, h, d, False)

    def do_back(t, h):
        for sgn in sgns:
            for d in dists:
                def test(n, sgn=sgn, d=d):
                    return d <= side(n, sgn, C)

                def sent(n, sgn=sgn, d=d):
                    root, nxt = n - sgn * d, n + sgn
                    return 0 <= nxt < C and parent(GATHER_TREES[t][h], side(C - 1 - root, sgn, C), d + 1) == d
                cond = among(lambda n: test(n) and not sent(n))
                if cond is not False:
                    when(cond, col_arrival(t, h, sgn, d).wait_recv)
        products(seg[t][h], row_of, 1, back[h], True)
        for i in range(1, hq + 1):
            for j in range(pt):
                pair_out[t][h][(i - 1) * pt + j] = back[h][links[3, (2 * i - 1) * pt + j]].astype(jnp.bfloat16)
            start(pair_copy(t, h, i))

    def return_row(t, h, d):
        arrival = pair_copy(t, h, d)
        if d < hq:
            slot = d - 1 + k
            view = tiles_at(pair_in[t][h], slot)
            to_row(view, view, t, h, half + 1 + slot, half + 1 + slot, partner).wait_recv()
        else:
            slot = d - 1 + k
            pl.when(k == 0)(arrival.wait_recv)
        for j in range(pt):
            value = back[h][links[3, 2 * d * pt + j]] + pair_in[t][h][slot * pt + j].astype(jnp.float32)
            row_out[t][h][(d - 1) * pt + j] = value.astype(jnp.bfloat16)
        start(row_copy(t, h, d))

    shift = center_ref[0]
    width = width_ref[0]

    def finish(t, h):
        pl.when(k == 1)(pair_copy(t, h, 1).wait_recv)
        for d in range(1, hq + 1):
            row_copy(t, h, d).wait_recv()
        for sgn in sgns:
            for d in dists:
                cond = final[t, h, sgn, d]
                if cond is not False:
                    when(cond, fin_arrival(t, h, sgn, d).wait_recv)
        slot = jnp.where(k == 1, 0, hq)
        for j in range(pt):
            total = back[h][links[3, j]] + direct[h][links[2, c * pt + j]]
            total += pair_in[t][h][slot * pt + j].astype(jnp.float32)
            for d in range(hq):
                total += row_in[t][h][d * pt + j].astype(jnp.float32)
            for sgn in sgns:
                for d in dists:
                    if final[t, h, sgn, d] is not False:
                        total += col_fin[t][h][way(sgn, d) * pt + j].astype(jnp.float32)
            begin = win[0][h][j].astype(jnp.float32)
            if t == 0:
                first = ((total - shift * begin) / width).astype(jnp.bfloat16)
                win[1][h][j] = first
                seg[1][h][c * pt + j] = first
            else:
                first = win[1][h][j].astype(jnp.float32)
                result[j, h * vc:(h + 1) * vc, :] = 2.0 * (total - shift * first) / width - begin

    def link_slots():
        count = counts_ref[0, 0]
        sub = lax.broadcasted_iota(jnp.int32, (slots, size), 0)
        lane = lax.broadcasted_iota(jnp.int32, (slots, size), 1)
        for i, keys in enumerate((row_of, col_of)):
            key = jnp.full((slots, size), -1, jnp.int32)
            column = key
            for s in range(slots):
                one = keys[0, s]
                key = jnp.where(lane == s, one, key)
                column = jnp.where(sub == s, one, column)
            used = sub < count
            same = (column == key) & (sub < lane) & used
            before = jnp.max(jnp.where(same, sub, -1), axis=0, keepdims=True)
            table[i:i + 1, :] = jnp.where(before < 0, slots, before)
            last = jnp.max(jnp.where((column == lane) & used, sub, -1), axis=0, keepdims=True)
            table[2 + i:3 + i, :] = jnp.where(last < 0, slots, last)
        publish = pltpu.make_async_copy(table, links, local.at[2])
        publish.start()
        publish.wait()

    def run(name, t, h):
        if name == "Gs":
            start_gather(t, h)
        elif name == "D":
            do_direct(t, h)
        elif name == "B":
            do_back(t, h)
        elif name == "E":
            finish(t, h)
        elif name[:2] == "RM":
            pass_on(t, h, int(name[2:]), True)
        else:
            {"XF": forward_row, "GF": forward_col, "RX": return_row}[name[:2]](t, h, int(name[2:]))

    linked = False
    for name, t, h in full_order(K, C, hq):
        if not linked and name in ("D", "B"):
            with SCOPE("link"):
                link_slots()
            linked = True
        if name in ("D", "B") and fetch is not None:
            fetch.wait()
            fetch = None
        with SCOPE("%s_%d%d" % (name, t, h)):
            run(name, t, h)
    with SCOPE("out"):
        for j in range(pt):
            out_ref[j * size:(j + 1) * size, :] = result[j].T.astype(jnp.bfloat16)
    with SCOPE("drain"):
        for copy, cond in drains:
            when(cond, copy.wait_send)


def per_device(start_vectors, tiles, tile_rows, tile_cols, tile_counts, center, half_width):
    R = lax.axis_size("row")
    C = lax.axis_size("col")
    half = R // 2
    hq = half // 2
    piece_rows, vec = start_vectors.shape
    size = tiles.shape[-1]
    slots = tiles.shape[1]
    pt = piece_rows // size
    vc = vec // CHUNKS
    ways = 2 * (C - 1)
    smem = pl.BlockSpec(memory_space=pltpu.SMEM)
    vmem = pl.BlockSpec(memory_space=pltpu.VMEM)
    anywhere = pl.BlockSpec(memory_space=pl.ANY)
    bf, f32, i32 = jnp.bfloat16, jnp.float32, jnp.int32

    def pair(count):
        return [pltpu.VMEM((count * pt, vc, size), bf) for _ in range(2 * CHUNKS)]

    scratch = (
        pair(half + 1) + pair(C) + pair(hq) + pair(hq) + pair(hq + 1) + pair(hq)
        + pair(ways) + pair(ways) + pair(ways)
        + [pltpu.VMEM((slots + 1, vc, size), f32) for _ in range(2 * CHUNKS)]
        + [
            pltpu.VMEM((piece_rows, vec), bf), pltpu.VMEM((pt, vec, size), f32),
            pltpu.VMEM((slots, size, size), bf),
            pltpu.VMEM((4, size), i32), pltpu.SMEM((4, size), i32),
            pltpu.SemaphoreType.DMA((3,)),
        ]
        + [pltpu.SemaphoreType.DMA((2, CHUNKS, half + 2 * hq + 1))] * 2
        + [pltpu.SemaphoreType.DMA((2, CHUNKS, 3 * ways))]
        + [pltpu.SemaphoreType.DMA((2, CHUNKS, C + 2 * ways))]
    )
    return pl.pallas_call(
        functools.partial(filter_kernel, (R, C, half, pt, slots, vec, size)),
        out_shape=jax.ShapeDtypeStruct((piece_rows, vec), bf),
        in_specs=[anywhere] * 2 + [smem] * 5,
        out_specs=vmem,
        scratch_shapes=scratch,
        compiler_params=pltpu.CompilerParams(
            collective_id=0, has_side_effects=True, vmem_limit_bytes=VMEM_LIMIT),
        name="filter_steps",
    )(start_vectors, tiles, tile_rows, tile_cols, tile_counts, center, half_width)


VMEM_LIMIT = 56_350_000


def solution(mesh):
    return jax.shard_map(
        per_device,
        mesh=mesh,
        in_specs=(
            P(("row", "col"), None),
            P("row", "col", None, None),
            P("row", "col"),
            P("row", "col"),
            P("row", "col"),
            P(),
            P(),
        ),
        out_specs=P(("row", "col"), None),
        check_vma=False,
    )
```

```python
import contextlib
import functools

import jax
import jax.numpy as jnp
from jax import lax
from jax.experimental import pallas as pl
from jax.experimental.pallas import tpu as pltpu
from jax.sharding import PartitionSpec as P

CHUNKS = 2
UNROLL = 16
MESH_ID = pl.DeviceIdType.MESH
GATHER_TREES = (("tail3", "tail3"), ("tail3", "tail"))
REDUCE_TREES = (("tail", "tail"), ("tail", "tail"))
ORDER = (
    "GX00", "GZ00", "GF200", "XF100", "GF100", "GF101", "GX01", "GZ01", "XF200", "D00",
    "XF101", "B00", "GF201", "RX00", "XF201", "D01", "RM100", "B01", "RX01", "RM200",
    "RM201", "RM101", "E00", "GX10", "GZ10", "E01", "XF110", "GX11", "GZ11", "XF210",
    "GF210", "D10", "GF110", "GF211", "XF111", "B10", "XF211", "GF111", "RM210", "D11",
    "RX10", "B11", "RM110", "RM211", "RX11", "RM111", "E10", "E11",
)
SCOPE = contextlib.nullcontext


def parent(kind, length, dist):
    if kind == "chain":
        return dist - 1
    if kind == "tail":
        return dist - 1 if dist == length and length >= 2 else 0
    if kind == "tail3":
        return dist - 1 if dist == length and length >= 3 else 0
    return 0


def side(c, sgn, C):
    return c if sgn > 0 else C - 1 - c


def forwards_at(C, t, h, n, sgn, d):
    root = n - sgn * d
    return (
        0 <= n < C and 0 <= root < C and 0 <= n + sgn < C
        and parent(GATHER_TREES[t][h], side(C - 1 - root, sgn, C), d + 1) == d)


def way_at(C, t, h, n, sgn, d):
    dest = n + sgn * d
    if not (0 <= n < C and 0 <= dest < C):
        return None
    kind, length = REDUCE_TREES[t][h], side(dest, sgn, C)
    return parent(kind, length, d), d < length and parent(kind, length, d + 1) == d


def passes_at(C, t, h, n, sgn, d):
    on = way_at(C, t, h, n, sgn, d)
    return on is not None and on[1]


def arrivals(C, K, hq):
    through, count = {}, 0
    for t in range(2):
        for h in range(K):
            at = hq + 4
            for kind, test in (("gather", forwards_at), ("reduce", passes_at)):
                for d in range(1, C - 1):
                    users = [{n for n in range(C) if test(C, t, h, n, sgn, d)} for sgn in (1, -1)]
                    through[t, h, kind, 1, d] = at
                    at += bool(users[0]) and bool(users[0] & users[1])
                    through[t, h, kind, -1, d] = at
                    at += bool(users[0] | users[1])
            count = max(count, at)
    return through, count


def default_order(K, C):
    order = []
    for h in range(K):
        order += [("GX", 0, h), ("GZ", 0, h)]
    for t in range(2):
        for h in range(K):
            order += [("XF1", t, h), ("XF2", t, h), ("GF1", t, h), ("D", t, h)]
        for h in range(K):
            order += [("GF2", t, h), ("RM2", t, h), ("RM1", t, h), ("B", t, h), ("RX", t, h)]
        for h in range(K):
            order.append(("E", t, h))
            if t == 0:
                order += [("GX", 1, h), ("GZ", 1, h)]
    return order


def full_order(K, C, hq):
    base = [(s[:-2], int(s[-2]), int(s[-1])) for s in ORDER] or default_order(K, C)
    known = set(base)
    order = []
    for name, t, h in base:
        extra = []
        if name == "D":
            extra = ["XF%d" % d for d in range(1, hq + 1)]
        elif name == "B":
            extra = ["GF%d" % d for d in range(1, C - 1)]
        elif name == "E":
            extra = ["RM%d" % d for d in range(C - 2, 0, -1)]
        order += [(e, t, h) for e in extra if (e, t, h) not in known]
        if name[:2] in ("XF", "GF", "RM") and int(name[2:]) > (hq if name[:2] == "XF" else C - 2):
            continue
        order.append((name, t, h))
    return order


def filter_kernel(
    dims, x_ref, tiles_ref, rows_ref, cols_ref, counts_ref, center_ref, width_ref, out_ref, *scratch,
):
    R, C, half, pt, slots, vec, size = dims
    K = CHUNKS
    vc = vec // K
    hq = half // 2
    ways = 2 * (C - 1)
    it = iter(scratch)

    def pair():
        return [[next(it) for _ in range(K)] for _ in range(2)]

    win, seg, pair_out, row_out, pair_in, row_in = pair(), pair(), pair(), pair(), pair(), pair()
    col_out, col_fin, col_mid = pair(), pair(), pair()
    back = [next(it) for _ in range(K)]
    direct = [next(it) for _ in range(K)]
    x_in, result, tiles, flipped, spare = next(it), next(it), next(it), next(it), next(it)
    table, row_of, col_of, links = next(it), next(it), next(it), next(it)
    local, sent, arrived = next(it), next(it), next(it)

    r = lax.axis_index("row")
    c = lax.axis_index("col")
    k = lax.rem(r, 2)
    partner = r + 1 - 2 * k

    def among(test):
        members = [n for n in range(C) if test(n)]
        if len(members) in (0, C):
            return members, bool(members)
        cond = None
        for lo in members:
            if lo - 1 in members:
                continue
            hi = lo
            while hi + 1 in members:
                hi += 1
            one = c == lo if lo == hi else c <= hi if lo == 0 else c >= lo if hi == C - 1 else (c >= lo) & (c <= hi)
            cond = one if cond is None else cond | one
        return members, cond

    everyone = (list(range(C)), True)

    def when(cond, act):
        if cond is True:
            act()
        elif cond is not False:
            pl.when(cond)(act)

    def pick(test, yes, no):
        cond = among(test)[1]
        return yes if cond is True else no if cond is False else jnp.where(cond, yes, no)

    forwards = functools.partial(forwards_at, C)
    way_on = functools.partial(way_at, C)
    EVEN, ODD, PAIR, LAST, PIECES = 0, hq, hq + 1, hq + 2, hq + 3
    through, _ = arrivals(C, K, hq)

    barrier = pltpu.get_barrier_semaphore()
    row_peers = sorted({d % R for d in range(2, half + 1, 2)} | {-d % R for d in range(2, half + 1, 2)})
    for off in row_peers:
        pl.semaphore_signal(barrier, inc=1, device_id={"row": lax.rem(r + off, R)}, device_id_type=MESH_ID)
    pl.semaphore_signal(barrier, inc=1, device_id={"row": partner}, device_id_type=MESH_ID)
    for off in range(1, C):
        pl.semaphore_signal(barrier, inc=1, device_id={"col": lax.rem(c + off, C)}, device_id_type=MESH_ID)

    load_x = pltpu.make_async_copy(x_ref, x_in, local.at[0])
    load_x.start()
    load_rows = pltpu.make_async_copy(rows_ref, row_of, local.at[3])
    load_rows.start()
    load_cols = pltpu.make_async_copy(cols_ref, col_of, local.at[4])
    load_cols.start()
    fetch = pltpu.make_async_copy(tiles_ref.at[0], tiles, local.at[1])
    fetch.start()

    def way(sgn, d):
        return 2 * (d - 1) + (0 if sgn > 0 else 1)

    def tiles_at(ref, slot):
        return ref.at[pl.ds(slot * pt, pt)]

    sgns = (1, -1)
    dists = range(1, C)
    final = {}
    for t in range(2):
        for h in range(K):
            for sgn in sgns:
                for d in dists:
                    members, cond = among(lambda n: way_on(t, h, n - sgn * d, sgn, d) is not None
                                          and way_on(t, h, n - sgn * d, sgn, d)[0] == 0)
                    final[t, h, sgn, d] = members, cond
                    if cond is not True and cond is not False:
                        def clear(t=t, h=h, sgn=sgn, d=d):
                            tiles_at(col_fin[t][h], way(sgn, d))[...] = jnp.zeros((pt, vc, size), jnp.bfloat16)
                        pl.when(jnp.logical_not(cond))(clear)
            tiles_at(pair_in[t][h], hq)[...] = jnp.zeros((pt, vc, size), jnp.bfloat16)
    for h in range(K):
        back[h][slots] = jnp.zeros((vc, size), jnp.float32)
        direct[h][slots] = jnp.zeros((vc, size), jnp.float32)

    with SCOPE("loadx"):
        load_x.wait()
    for j in range(pt):
        block = x_in[j * size:(j + 1) * size, :].astype(jnp.float32).T.astype(jnp.bfloat16)
        for h in range(K):
            part = block[h * vc:(h + 1) * vc, :]
            win[0][h][j] = part
            seg[0][h][c * pt + j] = part
    with SCOPE("greet"):
        pl.semaphore_wait(barrier, len(row_peers) + 1 + C - 1)

    sends = [0] * C

    def start(copy, whom=everyone):
        when(whom[1], copy.start)
        for n in whom[0]:
            sends[n] += 1

    def to_row(src, dst, t, h, sem, row):
        return pltpu.make_async_remote_copy(
            src_ref=src, dst_ref=dst, send_sem=sent, recv_sem=arrived.at[t, h, sem],
            device_id={"row": row}, device_id_type=MESH_ID)

    def to_col(src, dst, t, h, sem, col):
        return pltpu.make_async_remote_copy(
            src_ref=src, dst_ref=dst, send_sem=sent, recv_sem=arrived.at[t, h, sem],
            device_id={"col": col}, device_id_type=MESH_ID)

    def pieces(count):
        view = tiles_at(spare, 0) if count == 1 else spare.at[pl.ds(0, count * pt)]
        return view

    def await_pieces(t, h, sem, count):
        to_row(pieces(count), pieces(count), t, h, sem, partner).wait_recv()

    def by_count(counts, act):
        for count in sorted(set(counts) - {0}):
            when(among(lambda n: counts[n] == count)[1], lambda: act(count))

    def up(d):
        return lax.rem(r + d, R)

    def start_row(t, h):
        own = tiles_at(win[t][h], 0)
        for d in range(hq, 0, -1):
            start(to_row(own, tiles_at(win[t][h], 2 * d), t, h, EVEN + d - 1, up(R - 2 * d)))
        pl.when(k == 1)(to_row(own, tiles_at(win[t][h], 1), t, h, ODD, partner).start)

    def forward_row(t, h, d):
        await_pieces(t, h, EVEN + d - 1, 1)
        view = tiles_at(win[t][h], 2 * d)
        copy = to_row(view, tiles_at(win[t][h], 2 * d - 1 + 2 * k), t, h, ODD, partner)
        if d < hq:
            start(copy)
        else:
            pl.when(k == 0)(copy.start)
            for n in range(C):
                sends[n] += 1

    def col_piece(t, h, sgn, d, hop):
        view = tiles_at(seg[t][h], c - sgn * d)
        src = view if d else tiles_at(win[t][h], 0)
        sem = pick(lambda n: forwards(t, h, n + sgn * hop, sgn, d + hop),
                   through.get((t, h, "gather", sgn, d + hop), 0), PIECES)
        return to_col(src, view, t, h, sem, c + sgn * hop)

    def start_col(t, h):
        for hop in reversed(dists):
            for sgn in sgns:
                def test(n):
                    return 0 <= n + sgn * hop < C and parent(GATHER_TREES[t][h], side(C - 1 - n, sgn, C), hop) == 0
                whom = among(test)
                if whom[0]:
                    start(col_piece(t, h, sgn, 0, hop), whom)

    def forward_col(t, h, d):
        for sgn in sgns:
            whom = among(lambda n: forwards(t, h, n, sgn, d))
            if whom[0]:
                when(whom[1], lambda: await_pieces(t, h, through[t, h, "gather", sgn, d], 1))
                start(col_piece(t, h, sgn, d, 1), whom)

    def products(source, index_ref, link_row, sums, weights):
        def one(s, carry):
            term = lax.dot_general(
                source[index_ref[0, s]], weights[s], (((1,), (0,)), ((), ())),
                preferred_element_type=jnp.float32)
            sums[s] = sums[links[link_row, s]] + term
            return carry

        lax.fori_loop(0, slots, one, 0, unroll=UNROLL)

    def pass_on(t, h, d, want):
        for sgn in sgns:
            found = sorted({way_on(t, h, n, sgn, d) for n in range(C)} - {None})
            for left, helped in found:
                if helped != want:
                    continue
                whom = among(lambda n: way_on(t, h, n, sgn, d) == (left, helped))
                w = way(sgn, d)

                def act():
                    if helped:
                        await_pieces(t, h, through[t, h, "reduce", sgn, d], 1)
                    dest = c + sgn * d
                    for j in range(pt):
                        value = direct[h][links[2, dest * pt + j]]
                        if helped:
                            value += col_mid[t][h][w * pt + j].astype(jnp.float32)
                        col_out[t][h][w * pt + j] = value.astype(jnp.bfloat16)
                when(whom[1], act)
                src = tiles_at(col_out[t][h], w)
                if left == 0:
                    copy = to_col(src, tiles_at(col_fin[t][h], w), t, h, LAST, c + sgn * d)
                else:
                    copy = to_col(src, tiles_at(col_mid[t][h], way(sgn, left)), t, h,
                                  through[t, h, "reduce", sgn, left], c + sgn * (d - left))
                start(copy, whom)

    def do_direct(t, h):
        await_pieces(t, h, ODD, hq)
        products(win[t][h], col_of, 0, direct[h], flipped)
        for d in reversed(dists):
            pass_on(t, h, d, False)

    def do_back(t, h):
        held = [sum(forwards(t, h, n, sgn, d) for sgn in sgns for d in dists) for n in range(C)]
        by_count([C - 1 - held[n] for n in range(C)], lambda count: await_pieces(t, h, PIECES, count))
        products(seg[t][h], row_of, 1, back[h], tiles)
        for i in range(1, hq + 1):
            for j in range(pt):
                pair_out[t][h][(i - 1) * pt + j] = back[h][links[3, (2 * i - 1) * pt + j]].astype(jnp.bfloat16)
            start(to_row(tiles_at(pair_out[t][h], i - 1), tiles_at(pair_in[t][h], i - 1), t, h, PAIR, partner))

    def return_row(t, h):
        await_pieces(t, h, PAIR, hq)
        for d in range(hq, 0, -1):
            for j in range(pt):
                value = back[h][links[3, 2 * d * pt + j]] + pair_in[t][h][(d - 1 + k) * pt + j].astype(jnp.float32)
                row_out[t][h][(d - 1) * pt + j] = value.astype(jnp.bfloat16)
            start(to_row(tiles_at(row_out[t][h], d - 1), tiles_at(row_in[t][h], d - 1), t, h, LAST, up(2 * d)))

    shift = center_ref[0]
    width = width_ref[0]

    def finish(t, h):
        ends = [hq + sum(n in final[t, h, sgn, d][0] for sgn in sgns for d in dists) for n in range(C)]
        by_count(ends, lambda count: await_pieces(t, h, LAST, count))
        slot = jnp.where(k == 1, 0, hq)
        for j in range(pt):
            total = back[h][links[3, j]] + direct[h][links[2, c * pt + j]]
            total += pair_in[t][h][slot * pt + j].astype(jnp.float32)
            for d in range(hq):
                total += row_in[t][h][d * pt + j].astype(jnp.float32)
            for sgn in sgns:
                for d in dists:
                    if final[t, h, sgn, d][0]:
                        total += col_fin[t][h][way(sgn, d) * pt + j].astype(jnp.float32)
            begin = win[0][h][j].astype(jnp.float32)
            if t == 0:
                first = ((total - shift * begin) / width).astype(jnp.bfloat16)
                win[1][h][j] = first
                seg[1][h][c * pt + j] = first
            else:
                first = win[1][h][j].astype(jnp.float32)
                result[j, h * vc:(h + 1) * vc, :] = 2.0 * (total - shift * first) / width - begin

    def link_slots():
        load_rows.wait()
        load_cols.wait()
        count = counts_ref[0, 0]
        sub = lax.broadcasted_iota(jnp.int32, (slots, size), 0)
        lane = lax.broadcasted_iota(jnp.int32, (slots, size), 1)
        for i, keys in enumerate((row_of, col_of)):
            key = jnp.full((slots, size), -1, jnp.int32)
            column = key
            for s in range(slots):
                one = keys[0, s]
                key = jnp.where(lane == s, one, key)
                column = jnp.where(sub == s, one, column)
            used = sub < count
            same = (column == key) & (sub < lane) & used
            before = jnp.max(jnp.where(same, sub, -1), axis=0, keepdims=True)
            table[i:i + 1, :] = jnp.where(before < 0, slots, before)
            last = jnp.max(jnp.where((column == lane) & used, sub, -1), axis=0, keepdims=True)
            table[2 + i:3 + i, :] = jnp.where(last < 0, slots, last)
        publish = pltpu.make_async_copy(table, links, local.at[2])
        publish.start()
        fetch.wait()

        def flip(s, carry):
            flipped[s] = tiles[s].astype(jnp.float32).T.astype(jnp.bfloat16)
            return carry

        lax.fori_loop(0, slots, flip, 0, unroll=UNROLL)
        publish.wait()

    acts = {"GX": start_row, "GZ": start_col, "D": do_direct, "B": do_back, "RX": return_row, "E": finish}
    linked = 0
    for name, t, h in full_order(K, C, hq):
        with SCOPE("%s_%d%d" % (name, t, h)):
            if name in acts:
                acts[name](t, h)
            elif name[:2] == "RM":
                pass_on(t, h, int(name[2:]), True)
            else:
                (forward_row if name[:2] == "XF" else forward_col)(t, h, int(name[2:]))
        linked += (name, t, h) in (("GX", 0, 0), ("GZ", 0, 0))
        if linked == 2:
            with SCOPE("link"):
                link_slots()
            linked += 1
    with SCOPE("out"):
        for j in range(pt):
            out_ref[j * size:(j + 1) * size, :] = result[j].T.astype(jnp.bfloat16)
    with SCOPE("drain"):
        by_count(sends, lambda count: to_row(pieces(count), pieces(count), 0, 0, 0, partner).wait_send())


def per_device(start_vectors, tiles, tile_rows, tile_cols, tile_counts, center, half_width):
    R = lax.axis_size("row")
    C = lax.axis_size("col")
    half = R // 2
    hq = half // 2
    piece_rows, vec = start_vectors.shape
    size = tiles.shape[-1]
    slots = tiles.shape[1]
    pt = piece_rows // size
    vc = vec // CHUNKS
    ways = 2 * (C - 1)
    nsem = arrivals(C, CHUNKS, hq)[1]
    most = 2 * CHUNKS * (4 * hq + 4 * C)
    smem = pl.BlockSpec(memory_space=pltpu.SMEM)
    vmem = pl.BlockSpec(memory_space=pltpu.VMEM)
    anywhere = pl.BlockSpec(memory_space=pl.ANY)
    bf, f32, i32 = jnp.bfloat16, jnp.float32, jnp.int32

    def pair(count):
        return [pltpu.VMEM((count * pt, vc, size), bf) for _ in range(2 * CHUNKS)]

    scratch = (
        pair(half + 1) + pair(C) + pair(hq) + pair(hq) + pair(hq + 1) + pair(hq)
        + pair(ways) + pair(ways) + pair(ways)
        + [pltpu.VMEM((slots + 1, vc, size), f32) for _ in range(2 * CHUNKS)]
        + [
            pltpu.VMEM((piece_rows, vec), bf), pltpu.VMEM((pt, vec, size), f32),
            pltpu.VMEM((slots, size, size), bf), pltpu.VMEM((slots, size, size), bf),
            pltpu.VMEM((most * pt, vc, size), bf),
            pltpu.VMEM((4, size), i32),
            pltpu.SMEM((1, slots), i32), pltpu.SMEM((1, slots), i32), pltpu.SMEM((4, size), i32),
        ]
        + [pltpu.SemaphoreType.DMA((5,)), pltpu.SemaphoreType.DMA, pltpu.SemaphoreType.DMA((2, CHUNKS, nsem))]
    )
    return pl.pallas_call(
        functools.partial(filter_kernel, (R, C, half, pt, slots, vec, size)),
        out_shape=jax.ShapeDtypeStruct((piece_rows, vec), bf),
        in_specs=[anywhere] * 4 + [smem] * 3,
        out_specs=vmem,
        scratch_shapes=scratch,
        compiler_params=pltpu.CompilerParams(
            collective_id=0, has_side_effects=True, vmem_limit_bytes=VMEM_LIMIT),
        name="filter_steps",
    )(start_vectors, tiles, tile_rows, tile_cols, tile_counts, center, half_width)


VMEM_LIMIT = 56_350_000


def solution(mesh):
    return jax.shard_map(
        per_device,
        mesh=mesh,
        in_specs=(
            P(("row", "col"), None),
            P("row", "col", None, None),
            P("row", "col"),
            P("row", "col"),
            P("row", "col"),
            P(),
            P(),
        ),
        out_specs=P(("row", "col"), None),
        check_vma=False,
    )
```

```python
import contextlib
import functools

import jax
import jax.numpy as jnp
from jax import lax
from jax.experimental import pallas as pl
from jax.experimental.pallas import tpu as pltpu
from jax.sharding import PartitionSpec as P

CHUNKS = 2
UNROLL = 16
MESH_ID = pl.DeviceIdType.MESH
GATHER_TREES = (("tail3", "tail3"), ("tail3", "tail3"))
REDUCE_TREES = (("tail3", "tail"), ("tail", "tail"))
ORDER = (
    "GZ00", "GX00", "GF100", "GF101", "GZ01", "GF200", "GF201", "XF100", "GX01", "XF200",
    "D00", "B00", "XF201", "XF101", "RM200", "RX00", "RM100", "D01", "B01", "RM201",
    "RM101", "RX01", "E00", "GZ10", "GX10", "GF210", "E01", "GZ11", "GX11", "XF210",
    "XF110", "GF211", "D10", "GF110", "XF111", "B10", "XF211", "D11", "RM210", "RX10",
    "GF111", "B11", "RM110", "RM211", "RX11", "RM111", "E10", "E11",
)
SCOPE = contextlib.nullcontext


def parent(kind, length, dist):
    if kind == "chain":
        return dist - 1
    if kind == "tail":
        return dist - 1 if dist == length and length >= 2 else 0
    if kind == "tail3":
        return dist - 1 if dist == length and length >= 3 else 0
    return 0


def side(c, sgn, C):
    return c if sgn > 0 else C - 1 - c


def forwards_at(C, t, h, n, sgn, d):
    root = n - sgn * d
    return (
        0 <= n < C and 0 <= root < C and 0 <= n + sgn < C
        and parent(GATHER_TREES[t][h], side(C - 1 - root, sgn, C), d + 1) == d)


def way_at(C, t, h, n, sgn, d):
    dest = n + sgn * d
    if not (0 <= n < C and 0 <= dest < C):
        return None
    kind, length = REDUCE_TREES[t][h], side(dest, sgn, C)
    return parent(kind, length, d), d < length and parent(kind, length, d + 1) == d


def passes_at(C, t, h, n, sgn, d):
    on = way_at(C, t, h, n, sgn, d)
    return on is not None and on[1]


def arrivals(C, K, hq):
    through, count = {}, 0
    for t in range(2):
        for h in range(K):
            at = hq + 4
            for kind, test in (("gather", forwards_at), ("reduce", passes_at)):
                for d in range(1, C - 1):
                    users = [{n for n in range(C) if test(C, t, h, n, sgn, d)} for sgn in (1, -1)]
                    through[t, h, kind, 1, d] = at
                    at += bool(users[0]) and bool(users[0] & users[1])
                    through[t, h, kind, -1, d] = at
                    at += bool(users[0] | users[1])
            count = max(count, at)
    return through, count


def default_order(K, C):
    order = []
    for h in range(K):
        order += [("GX", 0, h), ("GZ", 0, h)]
    for t in range(2):
        for h in range(K):
            order += [("XF1", t, h), ("XF2", t, h), ("GF1", t, h), ("D", t, h)]
        for h in range(K):
            order += [("GF2", t, h), ("RM2", t, h), ("RM1", t, h), ("B", t, h), ("RX", t, h)]
        for h in range(K):
            order.append(("E", t, h))
            if t == 0:
                order += [("GX", 1, h), ("GZ", 1, h)]
    return order


def full_order(K, C, hq):
    base = [(s[:-2], int(s[-2]), int(s[-1])) for s in ORDER] or default_order(K, C)
    known = set(base)
    order = []
    for name, t, h in base:
        extra = []
        if name == "D":
            extra = ["XF%d" % d for d in range(1, hq + 1)]
        elif name == "B":
            extra = ["GF%d" % d for d in range(1, C - 1)]
        elif name == "E":
            extra = ["RM%d" % d for d in range(C - 2, 0, -1)]
        order += [(e, t, h) for e in extra if (e, t, h) not in known]
        if name[:2] in ("XF", "GF", "RM") and int(name[2:]) > (hq if name[:2] == "XF" else C - 2):
            continue
        order.append((name, t, h))
    return order


def filter_kernel(
    dims, x_ref, tiles_ref, rows_ref, cols_ref, counts_ref, center_ref, width_ref, out_ref, *scratch,
):
    R, C, half, pt, slots, vec, size = dims
    K = CHUNKS
    vc = vec // K
    hq = half // 2
    ways = 2 * (C - 1)
    it = iter(scratch)

    def pair():
        return [[next(it) for _ in range(K)] for _ in range(2)]

    win, seg, pair_out, row_out, pair_in, row_in = pair(), pair(), pair(), pair(), pair(), pair()
    col_out, col_fin, col_mid = pair(), pair(), pair()
    back = [next(it) for _ in range(K)]
    direct = [next(it) for _ in range(K)]
    x_in, result, tiles, flipped, spare = next(it), next(it), next(it), next(it), next(it)
    table, row_of, col_of, links = next(it), next(it), next(it), next(it)
    local, sent, arrived = next(it), next(it), next(it)

    r = lax.axis_index("row")
    c = lax.axis_index("col")
    k = lax.rem(r, 2)
    partner = r + 1 - 2 * k

    def among(test):
        members = [n for n in range(C) if test(n)]
        if len(members) in (0, C):
            return members, bool(members)
        cond = None
        for lo in members:
            if lo - 1 in members:
                continue
            hi = lo
            while hi + 1 in members:
                hi += 1
            one = c == lo if lo == hi else c <= hi if lo == 0 else c >= lo if hi == C - 1 else (c >= lo) & (c <= hi)
            cond = one if cond is None else cond | one
        return members, cond

    everyone = (list(range(C)), True)

    def when(cond, act):
        if cond is True:
            act()
        elif cond is not False:
            pl.when(cond)(act)

    def pick(test, yes, no):
        cond = among(test)[1]
        return yes if cond is True else no if cond is False else jnp.where(cond, yes, no)

    forwards = functools.partial(forwards_at, C)
    way_on = functools.partial(way_at, C)
    EVEN, ODD, PAIR, LAST, PIECES = 0, hq, hq + 1, hq + 2, hq + 3
    through, _ = arrivals(C, K, hq)

    barrier = pltpu.get_barrier_semaphore()
    row_peers = sorted({d % R for d in range(2, half + 1, 2)} | {-d % R for d in range(2, half + 1, 2)})
    for off in row_peers:
        pl.semaphore_signal(barrier, inc=1, device_id={"row": lax.rem(r + off, R)}, device_id_type=MESH_ID)
    pl.semaphore_signal(barrier, inc=1, device_id={"row": partner}, device_id_type=MESH_ID)
    for off in range(1, C):
        pl.semaphore_signal(barrier, inc=1, device_id={"col": lax.rem(c + off, C)}, device_id_type=MESH_ID)

    load_x = pltpu.make_async_copy(x_ref, x_in, local.at[0])
    load_x.start()
    load_rows = pltpu.make_async_copy(rows_ref, row_of, local.at[3])
    load_rows.start()
    load_cols = pltpu.make_async_copy(cols_ref, col_of, local.at[4])
    load_cols.start()
    fetch = pltpu.make_async_copy(tiles_ref.at[0], tiles, local.at[1])
    fetch.start()

    def way(sgn, d):
        return 2 * (d - 1) + (0 if sgn > 0 else 1)

    def tiles_at(ref, slot):
        return ref.at[pl.ds(slot * pt, pt)]

    sgns = (1, -1)
    dists = range(1, C)
    final = {}
    for t in range(2):
        for h in range(K):
            for sgn in sgns:
                for d in dists:
                    members, cond = among(lambda n: way_on(t, h, n - sgn * d, sgn, d) is not None
                                          and way_on(t, h, n - sgn * d, sgn, d)[0] == 0)
                    final[t, h, sgn, d] = members, cond
                    if cond is not True and cond is not False:
                        def clear(t=t, h=h, sgn=sgn, d=d):
                            tiles_at(col_fin[t][h], way(sgn, d))[...] = jnp.zeros((pt, vc, size), jnp.bfloat16)
                        pl.when(jnp.logical_not(cond))(clear)
            tiles_at(pair_in[t][h], hq)[...] = jnp.zeros((pt, vc, size), jnp.bfloat16)
    for h in range(K):
        back[h][slots] = jnp.zeros((vc, size), jnp.float32)
        direct[h][slots] = jnp.zeros((vc, size), jnp.float32)

    with SCOPE("loadx"):
        load_x.wait()
    for j in range(pt):
        block = x_in[j * size:(j + 1) * size, :].astype(jnp.float32).T.astype(jnp.bfloat16)
        for h in range(K):
            part = block[h * vc:(h + 1) * vc, :]
            win[0][h][j] = part
            seg[0][h][c * pt + j] = part
    with SCOPE("greet"):
        pl.semaphore_wait(barrier, len(row_peers) + 1 + C - 1)

    sends = [0] * C

    def start(copy, whom=everyone):
        when(whom[1], copy.start)
        for n in whom[0]:
            sends[n] += 1

    def to_row(src, dst, t, h, sem, row):
        return pltpu.make_async_remote_copy(
            src_ref=src, dst_ref=dst, send_sem=sent, recv_sem=arrived.at[t, h, sem],
            device_id={"row": row}, device_id_type=MESH_ID)

    def to_col(src, dst, t, h, sem, col):
        return pltpu.make_async_remote_copy(
            src_ref=src, dst_ref=dst, send_sem=sent, recv_sem=arrived.at[t, h, sem],
            device_id={"col": col}, device_id_type=MESH_ID)

    def pieces(count):
        view = tiles_at(spare, 0) if count == 1 else spare.at[pl.ds(0, count * pt)]
        return view

    def await_pieces(t, h, sem, count):
        to_row(pieces(count), pieces(count), t, h, sem, partner).wait_recv()

    def by_count(counts, act):
        for count in sorted(set(counts) - {0}):
            when(among(lambda n: counts[n] == count)[1], lambda: act(count))

    def up(d):
        return lax.rem(r + d, R)

    def start_row(t, h):
        own = tiles_at(win[t][h], 0)
        for d in range(hq, 0, -1):
            start(to_row(own, tiles_at(win[t][h], 2 * d), t, h, EVEN + d - 1, up(R - 2 * d)))
        pl.when(k == 1)(to_row(own, tiles_at(win[t][h], 1), t, h, ODD, partner).start)

    def forward_row(t, h, d):
        await_pieces(t, h, EVEN + d - 1, 1)
        view = tiles_at(win[t][h], 2 * d)
        copy = to_row(view, tiles_at(win[t][h], 2 * d - 1 + 2 * k), t, h, ODD, partner)
        if d < hq:
            start(copy)
        else:
            pl.when(k == 0)(copy.start)
            for n in range(C):
                sends[n] += 1

    def col_piece(t, h, sgn, d, hop):
        view = tiles_at(seg[t][h], c - sgn * d)
        src = view if d else tiles_at(win[t][h], 0)
        sem = pick(lambda n: forwards(t, h, n + sgn * hop, sgn, d + hop),
                   through.get((t, h, "gather", sgn, d + hop), 0), PIECES)
        return to_col(src, view, t, h, sem, c + sgn * hop)

    def start_col(t, h):
        for hop in reversed(dists):
            for sgn in sgns:
                def test(n):
                    return 0 <= n + sgn * hop < C and parent(GATHER_TREES[t][h], side(C - 1 - n, sgn, C), hop) == 0
                whom = among(test)
                if whom[0]:
                    start(col_piece(t, h, sgn, 0, hop), whom)

    def forward_col(t, h, d):
        for sgn in sgns:
            whom = among(lambda n: forwards(t, h, n, sgn, d))
            if whom[0]:
                when(whom[1], lambda: await_pieces(t, h, through[t, h, "gather", sgn, d], 1))
                start(col_piece(t, h, sgn, d, 1), whom)

    def products(source, index_ref, link_row, sums, weights):
        def one(s, carry):
            term = lax.dot_general(
                source[index_ref[0, s]], weights[s], (((1,), (0,)), ((), ())),
                preferred_element_type=jnp.float32)
            sums[s] = sums[links[link_row, s]] + term
            return carry

        lax.fori_loop(0, slots, one, 0, unroll=UNROLL)

    def pass_on(t, h, d, want):
        for sgn in sgns:
            found = sorted({way_on(t, h, n, sgn, d) for n in range(C)} - {None})
            for left, helped in found:
                if helped != want:
                    continue
                whom = among(lambda n: way_on(t, h, n, sgn, d) == (left, helped))
                w = way(sgn, d)

                def act():
                    if helped:
                        await_pieces(t, h, through[t, h, "reduce", sgn, d], 1)
                    dest = c + sgn * d
                    for j in range(pt):
                        value = direct[h][links[2, dest * pt + j]]
                        if helped:
                            value += col_mid[t][h][w * pt + j].astype(jnp.float32)
                        col_out[t][h][w * pt + j] = value.astype(jnp.bfloat16)
                when(whom[1], act)
                src = tiles_at(col_out[t][h], w)
                if left == 0:
                    copy = to_col(src, tiles_at(col_fin[t][h], w), t, h, LAST, c + sgn * d)
                else:
                    copy = to_col(src, tiles_at(col_mid[t][h], way(sgn, left)), t, h,
                                  through[t, h, "reduce", sgn, left], c + sgn * (d - left))
                start(copy, whom)

    def do_direct(t, h):
        await_pieces(t, h, ODD, hq)
        products(win[t][h], col_of, 0, direct[h], flipped)
        for d in reversed(dists):
            pass_on(t, h, d, False)

    def do_back(t, h):
        held = [sum(forwards(t, h, n, sgn, d) for sgn in sgns for d in dists) for n in range(C)]
        by_count([C - 1 - held[n] for n in range(C)], lambda count: await_pieces(t, h, PIECES, count))
        products(seg[t][h], row_of, 1, back[h], tiles)
        for i in range(1, hq + 1):
            for j in range(pt):
                pair_out[t][h][(i - 1) * pt + j] = back[h][links[3, (2 * i - 1) * pt + j]].astype(jnp.bfloat16)
            start(to_row(tiles_at(pair_out[t][h], i - 1), tiles_at(pair_in[t][h], i - 1), t, h, PAIR, partner))

    def return_row(t, h):
        await_pieces(t, h, PAIR, hq)
        for d in range(hq, 0, -1):
            for j in range(pt):
                value = back[h][links[3, 2 * d * pt + j]] + pair_in[t][h][(d - 1 + k) * pt + j].astype(jnp.float32)
                row_out[t][h][(d - 1) * pt + j] = value.astype(jnp.bfloat16)
            start(to_row(tiles_at(row_out[t][h], d - 1), tiles_at(row_in[t][h], d - 1), t, h, LAST, up(2 * d)))

    shift = center_ref[0]
    width = width_ref[0]

    def finish(t, h):
        ends = [hq + sum(n in final[t, h, sgn, d][0] for sgn in sgns for d in dists) for n in range(C)]
        by_count(ends, lambda count: await_pieces(t, h, LAST, count))
        slot = jnp.where(k == 1, 0, hq)
        for j in range(pt):
            total = back[h][links[3, j]] + direct[h][links[2, c * pt + j]]
            total += pair_in[t][h][slot * pt + j].astype(jnp.float32)
            for d in range(hq):
                total += row_in[t][h][d * pt + j].astype(jnp.float32)
            for sgn in sgns:
                for d in dists:
                    if final[t, h, sgn, d][0]:
                        total += col_fin[t][h][way(sgn, d) * pt + j].astype(jnp.float32)
            begin = win[0][h][j].astype(jnp.float32)
            if t == 0:
                first = ((total - shift * begin) / width).astype(jnp.bfloat16)
                win[1][h][j] = first
                seg[1][h][c * pt + j] = first
            else:
                first = win[1][h][j].astype(jnp.float32)
                result[j, h * vc:(h + 1) * vc, :] = 2.0 * (total - shift * first) / width - begin

    def link_slots():
        load_rows.wait()
        load_cols.wait()
        count = counts_ref[0, 0]
        sub = lax.broadcasted_iota(jnp.int32, (slots, size), 0)
        lane = lax.broadcasted_iota(jnp.int32, (slots, size), 1)
        for i, keys in enumerate((row_of, col_of)):
            key = jnp.full((slots, size), -1, jnp.int32)
            column = key
            for s in range(slots):
                one = keys[0, s]
                key = jnp.where(lane == s, one, key)
                column = jnp.where(sub == s, one, column)
            used = sub < count
            same = (column == key) & (sub < lane) & used
            before = jnp.max(jnp.where(same, sub, -1), axis=0, keepdims=True)
            table[i:i + 1, :] = jnp.where(before < 0, slots, before)
            last = jnp.max(jnp.where((column == lane) & used, sub, -1), axis=0, keepdims=True)
            table[2 + i:3 + i, :] = jnp.where(last < 0, slots, last)
        publish = pltpu.make_async_copy(table, links, local.at[2])
        publish.start()
        fetch.wait()

        def flip(s, carry):
            flipped[s] = tiles[s].astype(jnp.float32).T.astype(jnp.bfloat16)
            return carry

        lax.fori_loop(0, slots, flip, 0, unroll=UNROLL)
        publish.wait()

    acts = {"GX": start_row, "GZ": start_col, "D": do_direct, "B": do_back, "RX": return_row, "E": finish}
    linked = 0
    for name, t, h in full_order(K, C, hq):
        with SCOPE("%s_%d%d" % (name, t, h)):
            if name in acts:
                acts[name](t, h)
            elif name[:2] == "RM":
                pass_on(t, h, int(name[2:]), True)
            else:
                (forward_row if name[:2] == "XF" else forward_col)(t, h, int(name[2:]))
        linked += (name, t, h) in (("GX", 0, 0), ("GZ", 0, 0))
        if linked == 2:
            with SCOPE("link"):
                link_slots()
            linked += 1
    with SCOPE("out"):
        for j in range(pt):
            out_ref[j * size:(j + 1) * size, :] = result[j].T.astype(jnp.bfloat16)
    with SCOPE("drain"):
        by_count(sends, lambda count: to_row(pieces(count), pieces(count), 0, 0, 0, partner).wait_send())


def per_device(start_vectors, tiles, tile_rows, tile_cols, tile_counts, center, half_width):
    R = lax.axis_size("row")
    C = lax.axis_size("col")
    half = R // 2
    hq = half // 2
    piece_rows, vec = start_vectors.shape
    size = tiles.shape[-1]
    slots = tiles.shape[1]
    pt = piece_rows // size
    vc = vec // CHUNKS
    ways = 2 * (C - 1)
    nsem = arrivals(C, CHUNKS, hq)[1]
    most = 2 * CHUNKS * (4 * hq + 4 * C)
    smem = pl.BlockSpec(memory_space=pltpu.SMEM)
    vmem = pl.BlockSpec(memory_space=pltpu.VMEM)
    anywhere = pl.BlockSpec(memory_space=pl.ANY)
    bf, f32, i32 = jnp.bfloat16, jnp.float32, jnp.int32

    def pair(count):
        return [pltpu.VMEM((count * pt, vc, size), bf) for _ in range(2 * CHUNKS)]

    scratch = (
        pair(half + 1) + pair(C) + pair(hq) + pair(hq) + pair(hq + 1) + pair(hq)
        + pair(ways) + pair(ways) + pair(ways)
        + [pltpu.VMEM((slots + 1, vc, size), f32) for _ in range(2 * CHUNKS)]
        + [
            pltpu.VMEM((piece_rows, vec), bf), pltpu.VMEM((pt, vec, size), f32),
            pltpu.VMEM((slots, size, size), bf), pltpu.VMEM((slots, size, size), bf),
            pltpu.VMEM((most * pt, vc, size), bf),
            pltpu.VMEM((4, size), i32),
            pltpu.SMEM((1, slots), i32), pltpu.SMEM((1, slots), i32), pltpu.SMEM((4, size), i32),
        ]
        + [pltpu.SemaphoreType.DMA((5,)), pltpu.SemaphoreType.DMA, pltpu.SemaphoreType.DMA((2, CHUNKS, nsem))]
    )
    return pl.pallas_call(
        functools.partial(filter_kernel, (R, C, half, pt, slots, vec, size)),
        out_shape=jax.ShapeDtypeStruct((piece_rows, vec), bf),
        in_specs=[anywhere] * 4 + [smem] * 3,
        out_specs=vmem,
        scratch_shapes=scratch,
        compiler_params=pltpu.CompilerParams(
            collective_id=0, has_side_effects=True, vmem_limit_bytes=VMEM_LIMIT),
        name="filter_steps",
    )(start_vectors, tiles, tile_rows, tile_cols, tile_counts, center, half_width)


VMEM_LIMIT = 56_350_000


def solution(mesh):
    return jax.shard_map(
        per_device,
        mesh=mesh,
        in_specs=(
            P(("row", "col"), None),
            P("row", "col", None, None),
            P("row", "col"),
            P("row", "col"),
            P("row", "col"),
            P(),
            P(),
        ),
        out_specs=P(("row", "col"), None),
        check_vma=False,
    )
```

```python
import contextlib
import functools

import jax
import jax.numpy as jnp
from jax import lax
from jax.experimental import pallas as pl
from jax.experimental.pallas import tpu as pltpu
from jax.sharding import PartitionSpec as P

SHARES = (1, 1)
CHUNKS = len(SHARES)
GRAIN = 16
PARTS = 1
UNROLL = 16
MESH_ID = pl.DeviceIdType.MESH
GATHER_TREES = ((("tail3",), ("tail3",)), (("tail3",), ("tail3",)))
REDUCE_TREES = ((("tail",), ("tail",)), (("tail",), ("tail",)))
ORDER = (
    "GZ000", "GX00", "GZ001", "XF100", "GX01", "GF2S000", "XF200", "D00", "XF101", "XF201",
    "GF2S001", "D01", "RM1L000", "RM2L000", "B00", "RX00", "RM2L001", "B01", "RM1L001", "RX01",
    "E00", "GZ010", "GX10", "GF2S010", "E01", "GZ011", "GX11", "XF110", "XF210", "GF2S011",
    "D10", "XF111", "XF211", "B10", "D11", "RM1L010", "RX10", "RM2L010", "B11", "RM2L011",
    "RX11", "RM1L011", "E10", "E11",
)
SCOPE = contextlib.nullcontext


def widths(vec):
    return [vec * share // sum(SHARES) for share in SHARES]


def parts_of(pt):
    return PARTS if pt % PARTS == 0 else 1


def parent(kind, length, dist):
    if kind == "chain":
        return dist - 1
    if kind == "tail":
        return dist - 1 if dist == length and length >= 2 else 0
    if kind == "tail3":
        return dist - 1 if dist == length and length >= 3 else 0
    return 0


def side(c, sgn, C):
    return c if sgn > 0 else C - 1 - c


def is_long(C, n, sgn):
    return (2 * n < C) == (sgn > 0)


def forwards_at(C, t, h, u, n, sgn, d):
    root = n - sgn * d
    return (
        0 <= n < C and 0 <= root < C and 0 <= n + sgn < C
        and parent(GATHER_TREES[t][h][u], side(C - 1 - root, sgn, C), d + 1) == d)


def way_at(C, t, h, u, n, sgn, d):
    dest = n + sgn * d
    if not (0 <= n < C and 0 <= dest < C):
        return None
    kind, length = REDUCE_TREES[t][h][u], side(dest, sgn, C)
    return parent(kind, length, d), d < length and parent(kind, length, d + 1) == d


def passes_at(C, t, h, u, n, sgn, d):
    on = way_at(C, t, h, u, n, sgn, d)
    return on is not None and on[1]


def arrivals(C, K, hq, parts):
    through, count = {}, 0
    for t in range(2):
        for h in range(K):
            at = hq + 4
            for u in range(parts):
                for kind, test in (("gather", forwards_at), ("reduce", passes_at)):
                    for d in range(1, C - 1):
                        users = [{n for n in range(C) if test(C, t, h, u, n, sgn, d)} for sgn in (1, -1)]
                        through[t, h, u, kind, 1, d] = at
                        at += bool(users[0]) and bool(users[0] & users[1])
                        through[t, h, u, kind, -1, d] = at
                        at += bool(users[0] | users[1])
            count = max(count, at)
    return through, count


def parse(word):
    name, t, h = word[:-2], int(word[-2]), int(word[-1])
    kind = name[:2]
    if kind in ("XF", "GZ"):
        return kind, t, h, int(name[2:])
    if kind in ("GF", "RM"):
        return kind, t, h, int(name[2]), name[3], int(name[4])
    return name, t, h


def default_order(K, parts):
    order = []
    for h in range(K):
        order += [("GX", 0, h)] + [("GZ", 0, h, u) for u in range(parts)]
    for t in range(2):
        order += [("D", t, h) for h in range(K)]
        for h in range(K):
            order += [("B", t, h), ("RX", t, h)]
        for h in range(K):
            order.append(("E", t, h))
            if t == 0:
                order += [("GX", 1, h)] + [("GZ", 1, h, u) for u in range(parts)]
    return order


def full_order(K, C, hq, parts):
    base = [parse(word) for word in ORDER] or default_order(K, parts)
    known = set(base)
    order = []
    for task in base:
        kind, t, h = task[:3]
        extra = []
        if kind == "D":
            extra = [("XF", t, h, d) for d in range(1, hq + 1)]
        elif kind == "B":
            extra = [("GF", t, h, d, rel, u) for d in range(1, C - 1) for u in range(parts) for rel in "LS"]
        elif kind == "E":
            extra = [("RM", t, h, d, rel, u) for d in range(C - 2, 0, -1) for u in range(parts) for rel in "LS"]
        order += [e for e in extra if e not in known]
        if kind == "XF" and task[3] > hq or kind in ("GF", "RM") and task[3] > C - 2:
            continue
        if kind in ("GZ", "GF", "RM") and task[-1] >= parts:
            continue
        order.append(task)
    return order


def filter_kernel(
    dims, x_ref, tiles_ref, rows_ref, cols_ref, used_ref, shift_ref, scale_ref, out_ref, *scratch,
):
    R, C, half, pt, slots, vec, size = dims
    K = CHUNKS
    vcs = widths(vec)
    begins = [sum(vcs[:h]) for h in range(K)]
    hq = half // 2
    ways = 2 * (C - 1)
    parts = parts_of(pt)
    ptu = pt // parts
    it = iter(scratch)

    def pair():
        return [[next(it) for _ in range(K)] for _ in range(2)]

    win, seg, pair_out, row_out, pair_in, row_in = pair(), pair(), pair(), pair(), pair(), pair()
    col_out, col_fin, col_mid = pair(), pair(), pair()
    back = [next(it) for _ in range(K)]
    direct = [next(it) for _ in range(K)]
    x_in, result, tiles, flipped, spare = next(it), next(it), next(it), next(it), next(it)
    table, row_of, col_of = next(it), next(it), next(it)
    counts_ref, center_ref, width_ref, links = next(it), next(it), next(it), next(it)
    local, sent, arrived = next(it), next(it), next(it)

    r = lax.axis_index("row")
    c = lax.axis_index("col")
    k = lax.rem(r, 2)
    partner = r + 1 - 2 * k

    def among(test):
        members = [n for n in range(C) if test(n)]
        if len(members) in (0, C):
            return members, bool(members)
        cond = None
        for lo in members:
            if lo - 1 in members:
                continue
            hi = lo
            while hi + 1 in members:
                hi += 1
            one = c == lo if lo == hi else c <= hi if lo == 0 else c >= lo if hi == C - 1 else (c >= lo) & (c <= hi)
            cond = one if cond is None else cond | one
        return members, cond

    everyone = (list(range(C)), True)

    def when(cond, act):
        if cond is True:
            act()
        elif cond is not False:
            pl.when(cond)(act)

    def pick(test, yes, no):
        cond = among(test)[1]
        return yes if cond is True else no if cond is False else jnp.where(cond, yes, no)

    forwards = functools.partial(forwards_at, C)
    way_on = functools.partial(way_at, C)
    EVEN, ODD, PAIR, LAST, PIECES = 0, hq, hq + 1, hq + 2, hq + 3
    through, _ = arrivals(C, K, hq, parts)

    barrier = pltpu.get_barrier_semaphore()
    row_peers = sorted({d % R for d in range(2, half + 1, 2)} | {-d % R for d in range(2, half + 1, 2)})
    for off in row_peers:
        pl.semaphore_signal(barrier, inc=1, device_id={"row": lax.rem(r + off, R)}, device_id_type=MESH_ID)
    pl.semaphore_signal(barrier, inc=1, device_id={"row": partner}, device_id_type=MESH_ID)
    for off in range(1, C):
        pl.semaphore_signal(barrier, inc=1, device_id={"col": lax.rem(c + off, C)}, device_id_type=MESH_ID)

    load_x = pltpu.make_async_copy(x_ref, x_in, local.at[0])
    load_x.start()
    small = (
        (rows_ref, row_of), (cols_ref, col_of), (used_ref, counts_ref), (shift_ref, center_ref), (scale_ref, width_ref))
    loads = [pltpu.make_async_copy(src, dst, local.at[3 + i]) for i, (src, dst) in enumerate(small)]
    for copy in loads:
        copy.start()
    fetch = pltpu.make_async_copy(tiles_ref.at[0], tiles, local.at[1])
    fetch.start()

    def way(sgn, d):
        return 2 * (d - 1) + (0 if sgn > 0 else 1)

    def tiles_at(ref, slot):
        return ref.at[pl.ds(slot * pt, pt)]

    def part_at(ref, slot, u):
        return ref.at[pl.ds(slot * pt + u * ptu, ptu)]

    sgns = (1, -1)
    dists = range(1, C)
    final = {}
    for t in range(2):
        for h in range(K):
            for u in range(parts):
                for sgn in sgns:
                    for d in dists:
                        def test(n):
                            on = way_on(t, h, u, n - sgn * d, sgn, d)
                            return on is not None and on[0] == 0
                        members, cond = final[t, h, u, sgn, d] = among(test)
                        if cond is not True and cond is not False:
                            def clear():
                                part_at(col_fin[t][h], way(sgn, d), u)[...] = jnp.zeros(
                                    (ptu, vcs[h], size), jnp.bfloat16)
                            pl.when(jnp.logical_not(cond))(clear)
            tiles_at(pair_in[t][h], hq)[...] = jnp.zeros((pt, vcs[h], size), jnp.bfloat16)
    for h in range(K):
        back[h][slots] = jnp.zeros((vcs[h], size), jnp.float32)
        direct[h][slots] = jnp.zeros((vcs[h], size), jnp.float32)

    with SCOPE("loadx"):
        load_x.wait()
    for j in range(pt):
        block = x_in[j * size:(j + 1) * size, :].astype(jnp.float32).T.astype(jnp.bfloat16)
        for h in range(K):
            part = block[begins[h]:begins[h] + vcs[h], :]
            win[0][h][j] = part
            seg[0][h][c * pt + j] = part
    with SCOPE("greet"):
        pl.semaphore_wait(barrier, len(row_peers) + 1 + C - 1)

    sends = [0] * C

    def grains(count, h):
        return count * ptu * (vcs[h] // GRAIN)

    def start(copy, h, whom=everyone, count=parts):
        when(whom[1], copy.start)
        for n in whom[0]:
            sends[n] += grains(count, h)

    def to_row(src, dst, t, h, sem, row):
        return pltpu.make_async_remote_copy(
            src_ref=src, dst_ref=dst, send_sem=sent, recv_sem=arrived.at[t, h, sem],
            device_id={"row": row}, device_id_type=MESH_ID)

    def to_col(src, dst, t, h, sem, col):
        return pltpu.make_async_remote_copy(
            src_ref=src, dst_ref=dst, send_sem=sent, recv_sem=arrived.at[t, h, sem],
            device_id={"col": col}, device_id_type=MESH_ID)

    def await_pieces(t, h, sem, count):
        view = spare.at[pl.ds(0, grains(count, h))]
        to_row(view, view, t, h, sem, partner).wait_recv()

    def by_count(counts, act):
        for count in sorted(set(counts) - {0}):
            when(among(lambda n: counts[n] == count)[1], lambda: act(count))

    def up(d):
        return lax.rem(r + d, R)

    def start_row(t, h):
        own = tiles_at(win[t][h], 0)
        for d in range(hq, 0, -1):
            start(to_row(own, tiles_at(win[t][h], 2 * d), t, h, EVEN + d - 1, up(R - 2 * d)), h)
        pl.when(k == 1)(to_row(own, tiles_at(win[t][h], 1), t, h, ODD, partner).start)

    def forward_row(t, h, d):
        await_pieces(t, h, EVEN + d - 1, parts)
        view = tiles_at(win[t][h], 2 * d)
        copy = to_row(view, tiles_at(win[t][h], 2 * d - 1 + 2 * k), t, h, ODD, partner)
        if d < hq:
            start(copy, h)
        else:
            pl.when(k == 0)(copy.start)
            for n in range(C):
                sends[n] += grains(parts, h)

    def col_piece(t, h, u, sgn, d, hop):
        view = part_at(seg[t][h], c - sgn * d, u)
        src = view if d else part_at(win[t][h], 0, u)
        sem = pick(lambda n: forwards(t, h, u, n + sgn * hop, sgn, d + hop),
                   through.get((t, h, u, "gather", sgn, d + hop), 0), PIECES)
        return to_col(src, view, t, h, sem, c + sgn * hop)

    def start_col(t, h, u):
        for hop in reversed(dists):
            for sgn in sgns:
                def test(n):
                    return 0 <= n + sgn * hop < C and parent(GATHER_TREES[t][h][u], side(C - 1 - n, sgn, C), hop) == 0
                whom = among(test)
                if whom[0]:
                    start(col_piece(t, h, u, sgn, 0, hop), h, whom, 1)

    def forward_col(t, h, d, rel, u):
        for sgn in sgns:
            whom = among(lambda n: forwards(t, h, u, n, sgn, d) and is_long(C, n, sgn) == (rel == "L"))
            if whom[0]:
                when(whom[1], lambda: await_pieces(t, h, through[t, h, u, "gather", sgn, d], 1))
                start(col_piece(t, h, u, sgn, d, 1), h, whom, 1)

    def products(source, index_ref, link_row, sums, weights):
        def one(s, carry):
            term = lax.dot_general(
                source[index_ref[0, s]], weights[s], (((1,), (0,)), ((), ())),
                preferred_element_type=jnp.float32)
            sums[s] = sums[links[link_row, s]] + term
            return carry

        lax.fori_loop(0, slots, one, 0, unroll=UNROLL)

    def pass_on(t, h, d, rel, u):
        for sgn in sgns:
            found = sorted({way_on(t, h, u, n, sgn, d) for n in range(C)} - {None})
            for left, helped in found:
                if helped != bool(rel):
                    continue
                whom = among(lambda n: way_on(t, h, u, n, sgn, d) == (left, helped)
                             and (not rel or is_long(C, n, sgn) == (rel == "L")))
                if not whom[0]:
                    continue
                w = way(sgn, d)

                def act():
                    if helped:
                        await_pieces(t, h, through[t, h, u, "reduce", sgn, d], 1)
                    dest = c + sgn * d
                    for j in range(u * ptu, (u + 1) * ptu):
                        value = direct[h][links[2, dest * pt + j]]
                        if helped:
                            value += col_mid[t][h][w * pt + j].astype(jnp.float32)
                        col_out[t][h][w * pt + j] = value.astype(jnp.bfloat16)
                when(whom[1], act)
                src = part_at(col_out[t][h], w, u)
                if left == 0:
                    copy = to_col(src, part_at(col_fin[t][h], w, u), t, h, LAST, c + sgn * d)
                else:
                    copy = to_col(src, part_at(col_mid[t][h], way(sgn, left), u), t, h,
                                  through[t, h, u, "reduce", sgn, left], c + sgn * (d - left))
                start(copy, h, whom, 1)

    def do_direct(t, h):
        await_pieces(t, h, ODD, hq * parts)
        products(win[t][h], col_of, 0, direct[h], flipped)
        for u in range(parts):
            for d in reversed(dists):
                pass_on(t, h, d, "", u)

    def do_back(t, h):
        held = [sum(forwards(t, h, u, n, sgn, d) for u in range(parts) for sgn in sgns for d in dists) for n in range(C)]
        by_count([(C - 1) * parts - held[n] for n in range(C)], lambda count: await_pieces(t, h, PIECES, count))
        products(seg[t][h], row_of, 1, back[h], tiles)
        for i in range(1, hq + 1):
            for j in range(pt):
                pair_out[t][h][(i - 1) * pt + j] = back[h][links[3, (2 * i - 1) * pt + j]].astype(jnp.bfloat16)
            start(to_row(tiles_at(pair_out[t][h], i - 1), tiles_at(pair_in[t][h], i - 1), t, h, PAIR, partner), h)

    def return_row(t, h):
        await_pieces(t, h, PAIR, hq * parts)
        for d in range(hq, 0, -1):
            for j in range(pt):
                value = back[h][links[3, 2 * d * pt + j]] + pair_in[t][h][(d - 1 + k) * pt + j].astype(jnp.float32)
                row_out[t][h][(d - 1) * pt + j] = value.astype(jnp.bfloat16)
            start(to_row(tiles_at(row_out[t][h], d - 1), tiles_at(row_in[t][h], d - 1), t, h, LAST, up(2 * d)), h)


    def finish(t, h):
        ends = [hq * parts + sum(n in final[t, h, u, sgn, d][0] for u in range(parts) for sgn in sgns for d in dists)
                for n in range(C)]
        by_count(ends, lambda count: await_pieces(t, h, LAST, count))
        slot = jnp.where(k == 1, 0, hq)
        for j in range(pt):
            total = back[h][links[3, j]] + direct[h][links[2, c * pt + j]]
            total += pair_in[t][h][slot * pt + j].astype(jnp.float32)
            for d in range(hq):
                total += row_in[t][h][d * pt + j].astype(jnp.float32)
            for sgn in sgns:
                for d in dists:
                    if final[t, h, j // ptu, sgn, d][0]:
                        total += col_fin[t][h][way(sgn, d) * pt + j].astype(jnp.float32)
            begin = win[0][h][j].astype(jnp.float32)
            shift, width = center_ref[0], width_ref[0]
            if t == 0:
                first = ((total - shift * begin) / width).astype(jnp.bfloat16)
                win[1][h][j] = first
                seg[1][h][c * pt + j] = first
            else:
                first = win[1][h][j].astype(jnp.float32)
                result[j, begins[h]:begins[h] + vcs[h], :] = 2.0 * (total - shift * first) / width - begin

    def link_slots():
        for copy in loads:
            copy.wait()
        count = counts_ref[0, 0]
        sub = lax.broadcasted_iota(jnp.int32, (slots, size), 0)
        lane = lax.broadcasted_iota(jnp.int32, (slots, size), 1)
        for i, keys in enumerate((row_of, col_of)):
            key = jnp.full((slots, size), -1, jnp.int32)
            column = key
            for s in range(slots):
                one = keys[0, s]
                key = jnp.where(lane == s, one, key)
                column = jnp.where(sub == s, one, column)
            used = sub < count
            same = (column == key) & (sub < lane) & used
            before = jnp.max(jnp.where(same, sub, -1), axis=0, keepdims=True)
            table[i:i + 1, :] = jnp.where(before < 0, slots, before)
            last = jnp.max(jnp.where((column == lane) & used, sub, -1), axis=0, keepdims=True)
            table[2 + i:3 + i, :] = jnp.where(last < 0, slots, last)
        publish = pltpu.make_async_copy(table, links, local.at[2])
        publish.start()
        fetch.wait()

        def flip(s, carry):
            flipped[s] = tiles[s].astype(jnp.float32).T.astype(jnp.bfloat16)
            return carry

        lax.fori_loop(0, slots, flip, 0, unroll=UNROLL)
        publish.wait()

    acts = {
        "GX": start_row, "GZ": start_col, "XF": forward_row, "GF": forward_col, "D": do_direct, "RM": pass_on,
        "B": do_back, "RX": return_row, "E": finish}
    first = {("GX", 0, 0)} | {("GZ", 0, 0, u) for u in range(parts)}
    for kind, *args in full_order(K, C, hq, parts):
        with SCOPE(kind + "".join(str(a) for a in args)):
            acts[kind](*args)
        if first:
            first.discard((kind, *args))
            if not first:
                with SCOPE("link"):
                    link_slots()
    with SCOPE("out"):
        for j in range(pt):
            out_ref[j * size:(j + 1) * size, :] = result[j].T.astype(jnp.bfloat16)
    with SCOPE("drain"):
        def drained(count):
            view = spare.at[pl.ds(0, count)]
            to_row(view, view, 0, 0, 0, partner).wait_send()
        by_count(sends, drained)


def per_device(start_vectors, tiles, tile_rows, tile_cols, tile_counts, center, half_width):
    R = lax.axis_size("row")
    C = lax.axis_size("col")
    half = R // 2
    hq = half // 2
    piece_rows, vec = start_vectors.shape
    size = tiles.shape[-1]
    slots = tiles.shape[1]
    pt = piece_rows // size
    vcs = widths(vec)
    ways = 2 * (C - 1)
    parts = parts_of(pt)
    nsem = arrivals(C, CHUNKS, hq, parts)[1]
    most = 2 * (4 * hq + 4 * C) * pt * (vec // GRAIN)
    vmem = pl.BlockSpec(memory_space=pltpu.VMEM)
    bf, f32, i32 = jnp.bfloat16, jnp.float32, jnp.int32

    def pair(count):
        return [pltpu.VMEM((count * pt, vc, size), bf) for vc in vcs * 2]

    scratch = (
        pair(half + 1) + pair(C) + pair(hq) + pair(hq) + pair(hq + 1) + pair(hq)
        + pair(ways) + pair(ways) + pair(ways)
        + [pltpu.VMEM((slots + 1, vc, size), f32) for vc in vcs * 2]
        + [
            pltpu.VMEM((piece_rows, vec), bf), pltpu.VMEM((pt, vec, size), f32),
            pltpu.VMEM((slots, size, size), bf), pltpu.VMEM((slots, size, size), bf),
            pltpu.VMEM((most, GRAIN, size), bf),
            pltpu.VMEM((4, size), i32),
            pltpu.SMEM((1, slots), i32), pltpu.SMEM((1, slots), i32),
            pltpu.SMEM((1, 1), i32), pltpu.SMEM((1,), f32), pltpu.SMEM((1,), f32), pltpu.SMEM((4, size), i32),
        ]
        + [pltpu.SemaphoreType.DMA((8,)), pltpu.SemaphoreType.DMA, pltpu.SemaphoreType.DMA((2, CHUNKS, nsem))]
    )
    return pl.pallas_call(
        functools.partial(filter_kernel, (R, C, half, pt, slots, vec, size)),
        out_shape=jax.ShapeDtypeStruct((piece_rows, vec), bf),
        in_specs=[pl.BlockSpec(memory_space=pltpu.HBM)] * 4 + [pl.BlockSpec(memory_space=pl.ANY)] * 3,
        out_specs=vmem,
        scratch_shapes=scratch,
        compiler_params=pltpu.CompilerParams(
            collective_id=0, has_side_effects=True, vmem_limit_bytes=VMEM_LIMIT),
        name="filter_steps",
    )(*[pltpu.with_memory_space_constraint(a, pltpu.HBM) for a in (start_vectors, tiles, tile_rows, tile_cols)],
      tile_counts, center, half_width)


VMEM_LIMIT = 56_350_000


def solution(mesh):
    return jax.shard_map(
        per_device,
        mesh=mesh,
        in_specs=(
            P(("row", "col"), None),
            P("row", "col", None, None),
            P("row", "col"),
            P("row", "col"),
            P("row", "col"),
            P(),
            P(),
        ),
        out_specs=P(("row", "col"), None),
        check_vma=False,
    )
```

```python
import contextlib
import functools

import jax
import jax.numpy as jnp
from jax import lax
from jax.experimental import pallas as pl
from jax.experimental.pallas import tpu as pltpu
from jax.sharding import PartitionSpec as P

SHARES = (1, 1)
CHUNKS = len(SHARES)
GRAIN = 16
PARTS = 1
UNROLL = 16
MESH_ID = pl.DeviceIdType.MESH
GATHER_TREES = ((("tail3",), ("tail3",)), (("tail3",), ("tail3",)))
REDUCE_TREES = ((("tail3",), ("tail",)), (("tail3",), ("tail",)))
ORDER = (
    "GX00", "GZ000", "GZ001", "XF200", "GF2S000", "XF100", "GX01", "D00", "GF2S001", "XF101",
    "XF201", "D01", "RM2L000", "B00", "RX00", "RM2L001", "B01", "RM1L001", "RX01", "E00",
    "GZ010", "GX10", "GF2S010", "E01", "GZ011", "GX11", "XF110", "GF2S011", "XF210", "D10",
    "XF111", "XF211", "B10", "RM2L010", "D11", "RX10", "B11", "RM2L011", "RX11", "RM1L011",
    "E10", "E11",
)
SCOPE = contextlib.nullcontext


def widths(vec):
    return [vec * share // sum(SHARES) for share in SHARES]


def parts_of(pt):
    return PARTS if pt % PARTS == 0 else 1


def parent(kind, length, dist):
    if kind == "chain":
        return dist - 1
    if kind == "tail":
        return dist - 1 if dist == length and length >= 2 else 0
    if kind == "tail3":
        return dist - 1 if dist == length and length >= 3 else 0
    return 0


def side(c, sgn, C):
    return c if sgn > 0 else C - 1 - c


def is_long(C, n, sgn):
    return (2 * n < C) == (sgn > 0)


def forwards_at(C, t, h, u, n, sgn, d):
    root = n - sgn * d
    return (
        0 <= n < C and 0 <= root < C and 0 <= n + sgn < C
        and parent(GATHER_TREES[t][h][u], side(C - 1 - root, sgn, C), d + 1) == d)


def way_at(C, t, h, u, n, sgn, d):
    dest = n + sgn * d
    if not (0 <= n < C and 0 <= dest < C):
        return None
    kind, length = REDUCE_TREES[t][h][u], side(dest, sgn, C)
    return parent(kind, length, d), d < length and parent(kind, length, d + 1) == d


def passes_at(C, t, h, u, n, sgn, d):
    on = way_at(C, t, h, u, n, sgn, d)
    return on is not None and on[1]


def arrivals(C, K, hq, parts):
    through, count = {}, 0
    for t in range(2):
        for h in range(K):
            at = hq + 4
            for u in range(parts):
                for kind, test in (("gather", forwards_at), ("reduce", passes_at)):
                    for d in range(1, C - 1):
                        users = [{n for n in range(C) if test(C, t, h, u, n, sgn, d)} for sgn in (1, -1)]
                        through[t, h, u, kind, 1, d] = at
                        at += bool(users[0]) and bool(users[0] & users[1])
                        through[t, h, u, kind, -1, d] = at
                        at += bool(users[0] | users[1])
            count = max(count, at)
    return through, count


def line_hops(C, K, parts):
    hops = set()
    for t in range(2):
        for h in range(K):
            for u in range(parts):
                for n in range(C):
                    for sgn in (1, -1):
                        for d in range(1, C):
                            on = way_at(C, t, h, u, n, sgn, d)
                            if on is not None:
                                hops.add(d - on[0])
                            length = side(C - 1 - n, sgn, C)
                            if d <= length:
                                hops.add(d - parent(GATHER_TREES[t][h][u], length, d))
    return sorted(hops)


def parse(word):
    name, t, h = word[:-2], int(word[-2]), int(word[-1])
    kind = name[:2]
    if kind in ("XF", "GZ"):
        return kind, t, h, int(name[2:])
    if kind in ("GF", "RM"):
        return kind, t, h, int(name[2]), name[3], int(name[4])
    return name, t, h


def default_order(K, parts):
    order = []
    for h in range(K):
        order += [("GX", 0, h)] + [("GZ", 0, h, u) for u in range(parts)]
    for t in range(2):
        order += [("D", t, h) for h in range(K)]
        for h in range(K):
            order += [("B", t, h), ("RX", t, h)]
        for h in range(K):
            order.append(("E", t, h))
            if t == 0:
                order += [("GX", 1, h)] + [("GZ", 1, h, u) for u in range(parts)]
    return order


def full_order(K, C, hq, parts):
    base = [parse(word) for word in ORDER] or default_order(K, parts)
    known = set(base)
    order = []
    for task in base:
        kind, t, h = task[:3]
        extra = []
        if kind == "D":
            extra = [("XF", t, h, d) for d in range(1, hq + 1)]
        elif kind == "B":
            extra = [("GF", t, h, d, rel, u) for d in range(1, C - 1) for u in range(parts) for rel in "LS"]
        elif kind == "E":
            extra = [("RM", t, h, d, rel, u) for d in range(C - 2, 0, -1) for u in range(parts) for rel in "LS"]
        order += [e for e in extra if e not in known]
        if kind == "XF" and task[3] > hq or kind in ("GF", "RM") and task[3] > C - 2:
            continue
        if kind in ("GZ", "GF", "RM") and task[-1] >= parts:
            continue
        order.append(task)
    return order


def filter_kernel(
    dims, x_ref, tiles_ref, rows_ref, cols_ref, used_ref, shift_ref, scale_ref, out_ref, *scratch,
):
    R, C, half, pt, slots, vec, size = dims
    K = CHUNKS
    vcs = widths(vec)
    begins = [sum(vcs[:h]) for h in range(K)]
    hq = half // 2
    ways = 2 * (C - 1)
    parts = parts_of(pt)
    ptu = pt // parts
    it = iter(scratch)

    def pair():
        return [[next(it) for _ in range(K)] for _ in range(2)]

    win, seg, pair_out, row_out, pair_in, row_in = pair(), pair(), pair(), pair(), pair(), pair()
    col_out, col_fin, col_mid = pair(), pair(), pair()
    back = [next(it) for _ in range(K)]
    direct = [next(it) for _ in range(K)]
    x_in, result, tiles, flipped, spare = next(it), next(it), next(it), next(it), next(it)
    table, row_of, col_of = next(it), next(it), next(it)
    counts_ref, center_ref, width_ref, links = next(it), next(it), next(it), next(it)
    local, sent, arrived = next(it), next(it), next(it)

    r = lax.axis_index("row")
    c = lax.axis_index("col")
    k = lax.rem(r, 2)
    partner = r + 1 - 2 * k

    def among(test):
        members = [n for n in range(C) if test(n)]
        if len(members) in (0, C):
            return members, bool(members)
        cond = None
        for lo in members:
            if lo - 1 in members:
                continue
            hi = lo
            while hi + 1 in members:
                hi += 1
            one = c == lo if lo == hi else c <= hi if lo == 0 else c >= lo if hi == C - 1 else (c >= lo) & (c <= hi)
            cond = one if cond is None else cond | one
        return members, cond

    everyone = (list(range(C)), True)

    def when(cond, act):
        if cond is True:
            act()
        elif cond is not False:
            pl.when(cond)(act)

    def pick(test, yes, no):
        cond = among(test)[1]
        return yes if cond is True else no if cond is False else jnp.where(cond, yes, no)

    forwards = functools.partial(forwards_at, C)
    way_on = functools.partial(way_at, C)
    EVEN, ODD, PAIR, LAST, PIECES = 0, hq, hq + 1, hq + 2, hq + 3
    through, _ = arrivals(C, K, hq, parts)

    load_x = pltpu.make_async_copy(x_ref, x_in, local.at[0])
    load_x.start()
    barrier = pltpu.get_barrier_semaphore()
    row_peers = sorted({d % R for d in range(2, half + 1, 2)} | {-d % R for d in range(2, half + 1, 2)})
    for off in row_peers:
        pl.semaphore_signal(barrier, inc=1, device_id={"row": lax.rem(r + off, R)}, device_id_type=MESH_ID)
    pl.semaphore_signal(barrier, inc=1, device_id={"row": partner}, device_id_type=MESH_ID)
    greeted = len(row_peers) + 1
    for hop in range(1, C):
        for sgn in (1, -1):
            cond = among(lambda n: 0 <= n + sgn * hop < C)[1]

            def greet():
                pl.semaphore_signal(barrier, inc=1, device_id={"col": c + sgn * hop}, device_id_type=MESH_ID)
            when(cond, greet)
            greeted += int(cond) if isinstance(cond, bool) else jnp.where(cond, 1, 0)

    small = (
        (rows_ref, row_of), (cols_ref, col_of), (used_ref, counts_ref), (shift_ref, center_ref), (scale_ref, width_ref))
    loads = [pltpu.make_async_copy(src, dst, local.at[3 + i]) for i, (src, dst) in enumerate(small)]
    for copy in loads:
        copy.start()
    fetch = pltpu.make_async_copy(tiles_ref.at[0], tiles, local.at[1])
    fetch.start()

    def way(sgn, d):
        return 2 * (d - 1) + (0 if sgn > 0 else 1)

    def tiles_at(ref, slot):
        return ref.at[pl.ds(slot * pt, pt)]

    def part_at(ref, slot, u):
        return ref.at[pl.ds(slot * pt + u * ptu, ptu)]

    sgns = (1, -1)
    dists = range(1, C)
    final = {}
    for t in range(2):
        for h in range(K):
            for u in range(parts):
                for sgn in sgns:
                    for d in dists:
                        def test(n):
                            on = way_on(t, h, u, n - sgn * d, sgn, d)
                            return on is not None and on[0] == 0
                        final[t, h, u, sgn, d] = among(test)

    def clear():
        for (t, h, u, sgn, d), (_, cond) in final.items():
            if cond is not True and cond is not False:
                def zero():
                    part_at(col_fin[t][h], way(sgn, d), u)[...] = jnp.zeros((ptu, vcs[h], size), jnp.bfloat16)
                pl.when(jnp.logical_not(cond))(zero)
        for t in range(2):
            for h in range(K):
                tiles_at(pair_in[t][h], hq)[...] = jnp.zeros((pt, vcs[h], size), jnp.bfloat16)
        for h in range(K):
            back[h][slots] = jnp.zeros((vcs[h], size), jnp.float32)
            direct[h][slots] = jnp.zeros((vcs[h], size), jnp.float32)

    with SCOPE("loadx"):
        load_x.wait()
    for j in range(pt):
        block = x_in[j * size:(j + 1) * size, :].astype(jnp.float32).T.astype(jnp.bfloat16)
        for h in range(K):
            part = block[begins[h]:begins[h] + vcs[h], :]
            win[0][h][j] = part
            seg[0][h][c * pt + j] = part
    with SCOPE("greet"):
        pl.semaphore_wait(barrier, greeted)

    sends = [0] * C

    def grains(count, h):
        return count * ptu * (vcs[h] // GRAIN)

    def start(copy, h, whom=everyone, count=parts):
        when(whom[1], copy.start)
        for n in whom[0]:
            sends[n] += grains(count, h)

    def to_row(src, dst, t, h, sem, row):
        return pltpu.make_async_remote_copy(
            src_ref=src, dst_ref=dst, send_sem=sent, recv_sem=arrived.at[t, h, sem],
            device_id={"row": row}, device_id_type=MESH_ID)

    def to_col(src, dst, t, h, sem, col):
        return pltpu.make_async_remote_copy(
            src_ref=src, dst_ref=dst, send_sem=sent, recv_sem=arrived.at[t, h, sem],
            device_id={"col": col}, device_id_type=MESH_ID)

    def await_pieces(t, h, sem, count):
        view = spare.at[pl.ds(0, grains(count, h))]
        to_row(view, view, t, h, sem, partner).wait_recv()

    def by_count(counts, act):
        for count in sorted(set(counts) - {0}):
            when(among(lambda n: counts[n] == count)[1], lambda: act(count))

    def up(d):
        return lax.rem(r + d, R)

    def start_row(t, h):
        own = tiles_at(win[t][h], 0)
        for d in range(hq, 0, -1):
            start(to_row(own, tiles_at(win[t][h], 2 * d), t, h, EVEN + d - 1, up(R - 2 * d)), h)
        pl.when(k == 1)(to_row(own, tiles_at(win[t][h], 1), t, h, ODD, partner).start)

    def forward_row(t, h, d):
        await_pieces(t, h, EVEN + d - 1, parts)
        view = tiles_at(win[t][h], 2 * d)
        copy = to_row(view, tiles_at(win[t][h], 2 * d - 1 + 2 * k), t, h, ODD, partner)
        if d < hq:
            start(copy, h)
        else:
            pl.when(k == 0)(copy.start)
            for n in range(C):
                sends[n] += grains(parts, h)

    def col_piece(t, h, u, sgn, d, hop):
        view = part_at(seg[t][h], c - sgn * d, u)
        src = view if d else part_at(win[t][h], 0, u)
        sem = pick(lambda n: forwards(t, h, u, n + sgn * hop, sgn, d + hop),
                   through.get((t, h, u, "gather", sgn, d + hop), 0), PIECES)
        return to_col(src, view, t, h, sem, c + sgn * hop)

    def start_col(t, h, u):
        for hop in reversed(dists):
            for sgn in sgns:
                def test(n):
                    return 0 <= n + sgn * hop < C and parent(GATHER_TREES[t][h][u], side(C - 1 - n, sgn, C), hop) == 0
                whom = among(test)
                if whom[0]:
                    start(col_piece(t, h, u, sgn, 0, hop), h, whom, 1)

    def forward_col(t, h, d, rel, u):
        for sgn in sgns:
            whom = among(lambda n: forwards(t, h, u, n, sgn, d) and is_long(C, n, sgn) == (rel == "L"))
            if whom[0]:
                when(whom[1], lambda: await_pieces(t, h, through[t, h, u, "gather", sgn, d], 1))
                start(col_piece(t, h, u, sgn, d, 1), h, whom, 1)

    def products(source, index_ref, link_row, sums, weights):
        def one(s, carry):
            term = lax.dot_general(
                source[index_ref[0, s]], weights[s], (((1,), (0,)), ((), ())),
                preferred_element_type=jnp.float32)
            sums[s] = sums[links[link_row, s]] + term
            return carry

        lax.fori_loop(0, slots, one, 0, unroll=UNROLL)

    def pass_on(t, h, d, rel, u):
        for sgn in sgns:
            found = sorted({way_on(t, h, u, n, sgn, d) for n in range(C)} - {None})
            for left, helped in found:
                if helped != bool(rel):
                    continue
                whom = among(lambda n: way_on(t, h, u, n, sgn, d) == (left, helped)
                             and (not rel or is_long(C, n, sgn) == (rel == "L")))
                if not whom[0]:
                    continue
                w = way(sgn, d)

                def act():
                    if helped:
                        await_pieces(t, h, through[t, h, u, "reduce", sgn, d], 1)
                    dest = c + sgn * d
                    for j in range(u * ptu, (u + 1) * ptu):
                        value = direct[h][links[2, dest * pt + j]]
                        if helped:
                            value += col_mid[t][h][w * pt + j].astype(jnp.float32)
                        col_out[t][h][w * pt + j] = value.astype(jnp.bfloat16)
                when(whom[1], act)
                src = part_at(col_out[t][h], w, u)
                if left == 0:
                    copy = to_col(src, part_at(col_fin[t][h], w, u), t, h, LAST, c + sgn * d)
                else:
                    copy = to_col(src, part_at(col_mid[t][h], way(sgn, left), u), t, h,
                                  through[t, h, u, "reduce", sgn, left], c + sgn * (d - left))
                start(copy, h, whom, 1)

    def do_direct(t, h):
        await_pieces(t, h, ODD, hq * parts)
        products(win[t][h], col_of, 0, direct[h], flipped)
        for u in range(parts):
            for d in reversed(dists):
                pass_on(t, h, d, "", u)

    def do_back(t, h):
        held = [sum(forwards(t, h, u, n, sgn, d) for u in range(parts) for sgn in sgns for d in dists) for n in range(C)]
        by_count([(C - 1) * parts - held[n] for n in range(C)], lambda count: await_pieces(t, h, PIECES, count))
        products(seg[t][h], row_of, 1, back[h], tiles)
        for i in range(1, hq + 1):
            for j in range(pt):
                pair_out[t][h][(i - 1) * pt + j] = back[h][links[3, (2 * i - 1) * pt + j]].astype(jnp.bfloat16)
            start(to_row(tiles_at(pair_out[t][h], i - 1), tiles_at(pair_in[t][h], i - 1), t, h, PAIR, partner), h)

    def return_row(t, h):
        await_pieces(t, h, PAIR, hq * parts)
        for d in range(hq, 0, -1):
            for j in range(pt):
                value = back[h][links[3, 2 * d * pt + j]] + pair_in[t][h][(d - 1 + k) * pt + j].astype(jnp.float32)
                row_out[t][h][(d - 1) * pt + j] = value.astype(jnp.bfloat16)
            start(to_row(tiles_at(row_out[t][h], d - 1), tiles_at(row_in[t][h], d - 1), t, h, LAST, up(2 * d)), h)


    def finish(t, h):
        ends = [hq * parts + sum(n in final[t, h, u, sgn, d][0] for u in range(parts) for sgn in sgns for d in dists)
                for n in range(C)]
        by_count(ends, lambda count: await_pieces(t, h, LAST, count))
        slot = jnp.where(k == 1, 0, hq)
        for j in range(pt):
            total = back[h][links[3, j]] + direct[h][links[2, c * pt + j]]
            total += pair_in[t][h][slot * pt + j].astype(jnp.float32)
            for d in range(hq):
                total += row_in[t][h][d * pt + j].astype(jnp.float32)
            for sgn in sgns:
                for d in dists:
                    if final[t, h, j // ptu, sgn, d][0]:
                        total += col_fin[t][h][way(sgn, d) * pt + j].astype(jnp.float32)
            begin = win[0][h][j].astype(jnp.float32)
            shift, width = center_ref[0], width_ref[0]
            if t == 0:
                first = ((total - shift * begin) / width).astype(jnp.bfloat16)
                win[1][h][j] = first
                seg[1][h][c * pt + j] = first
            else:
                first = win[1][h][j].astype(jnp.float32)
                result[j, begins[h]:begins[h] + vcs[h], :] = 2.0 * (total - shift * first) / width - begin

    def link_slots():
        for copy in loads:
            copy.wait()
        count = counts_ref[0, 0]
        sub = lax.broadcasted_iota(jnp.int32, (slots, size), 0)
        lane = lax.broadcasted_iota(jnp.int32, (slots, size), 1)
        for i, keys in enumerate((row_of, col_of)):
            key = jnp.full((slots, size), -1, jnp.int32)
            column = key
            for s in range(slots):
                one = keys[0, s]
                key = jnp.where(lane == s, one, key)
                column = jnp.where(sub == s, one, column)
            used = sub < count
            same = (column == key) & (sub < lane) & used
            before = jnp.max(jnp.where(same, sub, -1), axis=0, keepdims=True)
            table[i:i + 1, :] = jnp.where(before < 0, slots, before)
            last = jnp.max(jnp.where((column == lane) & used, sub, -1), axis=0, keepdims=True)
            table[2 + i:3 + i, :] = jnp.where(last < 0, slots, last)
        publish = pltpu.make_async_copy(table, links, local.at[2])
        publish.start()
        fetch.wait()

        def flip(s, carry):
            flipped[s] = tiles[s].astype(jnp.float32).T.astype(jnp.bfloat16)
            return carry

        lax.fori_loop(0, slots, flip, 0, unroll=UNROLL)
        publish.wait()

    acts = {
        "GX": start_row, "GZ": start_col, "XF": forward_row, "GF": forward_col, "D": do_direct, "RM": pass_on,
        "B": do_back, "RX": return_row, "E": finish}
    first = {("GX", 0, 0)} | {("GZ", 0, 0, u) for u in range(parts)}
    for kind, *args in full_order(K, C, hq, parts):
        with SCOPE(kind + "".join(str(a) for a in args)):
            acts[kind](*args)
        if first:
            first.discard((kind, *args))
            if not first:
                with SCOPE("link"):
                    clear()
                    link_slots()
    with SCOPE("out"):
        for j in range(pt):
            out_ref[j * size:(j + 1) * size, :] = result[j].T.astype(jnp.bfloat16)
    with SCOPE("drain"):
        def drained(count):
            view = spare.at[pl.ds(0, count)]
            to_row(view, view, 0, 0, 0, partner).wait_send()
        by_count(sends, drained)


def per_device(start_vectors, tiles, tile_rows, tile_cols, tile_counts, center, half_width):
    R = lax.axis_size("row")
    C = lax.axis_size("col")
    half = R // 2
    hq = half // 2
    piece_rows, vec = start_vectors.shape
    size = tiles.shape[-1]
    slots = tiles.shape[1]
    pt = piece_rows // size
    vcs = widths(vec)
    ways = 2 * (C - 1)
    parts = parts_of(pt)
    nsem = arrivals(C, CHUNKS, hq, parts)[1]
    most = 2 * (4 * hq + 4 * C) * pt * (vec // GRAIN)
    vmem = pl.BlockSpec(memory_space=pltpu.VMEM)
    bf, f32, i32 = jnp.bfloat16, jnp.float32, jnp.int32

    def pair(count):
        return [pltpu.VMEM((count * pt, vc, size), bf) for vc in vcs * 2]

    scratch = (
        pair(half + 1) + pair(C) + pair(hq) + pair(hq) + pair(hq + 1) + pair(hq)
        + pair(ways) + pair(ways) + pair(ways)
        + [pltpu.VMEM((slots + 1, vc, size), f32) for vc in vcs * 2]
        + [
            pltpu.VMEM((piece_rows, vec), bf), pltpu.VMEM((pt, vec, size), f32),
            pltpu.VMEM((slots, size, size), bf), pltpu.VMEM((slots, size, size), bf),
            pltpu.VMEM((most, GRAIN, size), bf),
            pltpu.VMEM((4, size), i32),
            pltpu.SMEM((1, slots), i32), pltpu.SMEM((1, slots), i32),
            pltpu.SMEM((1, 1), i32), pltpu.SMEM((1,), f32), pltpu.SMEM((1,), f32), pltpu.SMEM((4, size), i32),
        ]
        + [pltpu.SemaphoreType.DMA((8,)), pltpu.SemaphoreType.DMA, pltpu.SemaphoreType.DMA((2, CHUNKS, nsem))]
    )
    return pl.pallas_call(
        functools.partial(filter_kernel, (R, C, half, pt, slots, vec, size)),
        out_shape=jax.ShapeDtypeStruct((piece_rows, vec), bf),
        in_specs=[pl.BlockSpec(memory_space=pltpu.HBM)] * 4 + [pl.BlockSpec(memory_space=pl.ANY)] * 3,
        out_specs=vmem,
        scratch_shapes=scratch,
        compiler_params=pltpu.CompilerParams(
            collective_id=0, has_side_effects=True, vmem_limit_bytes=VMEM_LIMIT),
        name="filter_steps",
    )(*[pltpu.with_memory_space_constraint(a, pltpu.HBM) for a in (start_vectors, tiles, tile_rows, tile_cols)],
      tile_counts, center, half_width)


VMEM_LIMIT = 48 << 20


def solution(mesh):
    return jax.shard_map(
        per_device,
        mesh=mesh,
        in_specs=(
            P(("row", "col"), None),
            P("row", "col", None, None),
            P("row", "col"),
            P("row", "col"),
            P("row", "col"),
            P(),
            P(),
        ),
        out_specs=P(("row", "col"), None),
        check_vma=False,
    )
```

```python
import contextlib
import functools

import jax
import jax.numpy as jnp
from jax import lax
from jax.experimental import pallas as pl
from jax.experimental.pallas import tpu as pltpu
from jax.sharding import PartitionSpec as P

SHARES = (1, 1)
CHUNKS = len(SHARES)
GRAIN = 16
PARTS = 1
UNROLL = 32
MESH_ID = pl.DeviceIdType.MESH
GATHER_TREES = ((("tail3",), ("tail3",)), (("tail3",), ("tail3",)))
REDUCE_TREES = ((("tail3",), ("tail",)), (("tail3",), ("tail",)))
ORDER = (
    "GX00", "GZ000", "GZ001", "XF200", "GF2S000", "XF100", "GX01", "D00", "GF2S001", "XF101",
    "XF201", "D01", "RM2L000", "B00", "RX00", "RM2L001", "B01", "RM1L001", "RX01", "E00",
    "GZ010", "GX10", "GF2S010", "E01", "GZ011", "GX11", "XF110", "GF2S011", "XF210", "D10",
    "XF111", "XF211", "B10", "RM2L010", "D11", "RX10", "B11", "RM2L011", "RX11", "RM1L011",
    "E10", "E11",
)
SCOPE = contextlib.nullcontext


def widths(vec):
    return [vec * share // sum(SHARES) for share in SHARES]


def parts_of(pt):
    return PARTS if pt % PARTS == 0 else 1


def parent(kind, length, dist):
    if kind == "chain":
        return dist - 1
    if kind == "tail":
        return dist - 1 if dist == length and length >= 2 else 0
    if kind == "tail3":
        return dist - 1 if dist == length and length >= 3 else 0
    return 0


def side(c, sgn, C):
    return c if sgn > 0 else C - 1 - c


def is_long(C, n, sgn):
    return (2 * n < C) == (sgn > 0)


def forwards_at(C, t, h, u, n, sgn, d):
    root = n - sgn * d
    return (
        0 <= n < C and 0 <= root < C and 0 <= n + sgn < C
        and parent(GATHER_TREES[t][h][u], side(C - 1 - root, sgn, C), d + 1) == d)


def way_at(C, t, h, u, n, sgn, d):
    dest = n + sgn * d
    if not (0 <= n < C and 0 <= dest < C):
        return None
    kind, length = REDUCE_TREES[t][h][u], side(dest, sgn, C)
    return parent(kind, length, d), d < length and parent(kind, length, d + 1) == d


def passes_at(C, t, h, u, n, sgn, d):
    on = way_at(C, t, h, u, n, sgn, d)
    return on is not None and on[1]


def arrivals(C, K, hq, parts):
    through, count = {}, 0
    for t in range(2):
        for h in range(K):
            at = hq + 4
            for u in range(parts):
                for kind, test in (("gather", forwards_at), ("reduce", passes_at)):
                    for d in range(1, C - 1):
                        users = [{n for n in range(C) if test(C, t, h, u, n, sgn, d)} for sgn in (1, -1)]
                        through[t, h, u, kind, 1, d] = at
                        at += bool(users[0]) and bool(users[0] & users[1])
                        through[t, h, u, kind, -1, d] = at
                        at += bool(users[0] | users[1])
            count = max(count, at)
    return through, count


def line_hops(C, K, parts):
    hops = set()
    for t in range(2):
        for h in range(K):
            for u in range(parts):
                for n in range(C):
                    for sgn in (1, -1):
                        for d in range(1, C):
                            on = way_at(C, t, h, u, n, sgn, d)
                            if on is not None:
                                hops.add(d - on[0])
                            length = side(C - 1 - n, sgn, C)
                            if d <= length:
                                hops.add(d - parent(GATHER_TREES[t][h][u], length, d))
    return sorted(hops)


def parse(word):
    name, t, h = word[:-2], int(word[-2]), int(word[-1])
    kind = name[:2]
    if kind in ("XF", "GZ"):
        return kind, t, h, int(name[2:])
    if kind in ("GF", "RM"):
        return kind, t, h, int(name[2]), name[3], int(name[4])
    return name, t, h


def default_order(K, parts):
    order = []
    for h in range(K):
        order += [("GX", 0, h)] + [("GZ", 0, h, u) for u in range(parts)]
    for t in range(2):
        order += [("D", t, h) for h in range(K)]
        for h in range(K):
            order += [("B", t, h), ("RX", t, h)]
        for h in range(K):
            order.append(("E", t, h))
            if t == 0:
                order += [("GX", 1, h)] + [("GZ", 1, h, u) for u in range(parts)]
    return order


def full_order(K, C, hq, parts):
    base = [parse(word) for word in ORDER] or default_order(K, parts)
    known = set(base)
    order = []
    for task in base:
        kind, t, h = task[:3]
        extra = []
        if kind == "D":
            extra = [("XF", t, h, d) for d in range(1, hq + 1)]
        elif kind == "B":
            extra = [("GF", t, h, d, rel, u) for d in range(1, C - 1) for u in range(parts) for rel in "LS"]
        elif kind == "E":
            extra = [("RM", t, h, d, rel, u) for d in range(C - 2, 0, -1) for u in range(parts) for rel in "LS"]
        order += [e for e in extra if e not in known]
        if kind == "XF" and task[3] > hq or kind in ("GF", "RM") and task[3] > C - 2:
            continue
        if kind in ("GZ", "GF", "RM") and task[-1] >= parts:
            continue
        order.append(task)
    return order


def filter_kernel(
    dims, x_ref, tiles_ref, rows_ref, cols_ref, used_ref, shift_ref, scale_ref, out_ref, *scratch,
):
    R, C, half, pt, slots, vec, size = dims
    K = CHUNKS
    vcs = widths(vec)
    begins = [sum(vcs[:h]) for h in range(K)]
    hq = half // 2
    ways = 2 * (C - 1)
    parts = parts_of(pt)
    ptu = pt // parts
    it = iter(scratch)

    def pair():
        return [[next(it) for _ in range(K)] for _ in range(2)]

    win, seg, pair_out, row_out, pair_in, row_in = pair(), pair(), pair(), pair(), pair(), pair()
    col_out, col_fin, col_mid = pair(), pair(), pair()
    back = [next(it) for _ in range(K)]
    direct = [next(it) for _ in range(K)]
    x_in, result, tiles, flipped, spare = next(it), next(it), next(it), next(it), next(it)
    table, row_of, col_of = next(it), next(it), next(it)
    counts_ref, center_ref, width_ref, links = next(it), next(it), next(it), next(it)
    local, sent, arrived = next(it), next(it), next(it)

    r = lax.axis_index("row")
    c = lax.axis_index("col")
    k = lax.rem(r, 2)
    partner = r + 1 - 2 * k

    def among(test):
        members = [n for n in range(C) if test(n)]
        if len(members) in (0, C):
            return members, bool(members)
        cond = None
        for lo in members:
            if lo - 1 in members:
                continue
            hi = lo
            while hi + 1 in members:
                hi += 1
            one = c == lo if lo == hi else c <= hi if lo == 0 else c >= lo if hi == C - 1 else (c >= lo) & (c <= hi)
            cond = one if cond is None else cond | one
        return members, cond

    everyone = (list(range(C)), True)

    def when(cond, act):
        if cond is True:
            act()
        elif cond is not False:
            pl.when(cond)(act)

    def pick(test, yes, no):
        cond = among(test)[1]
        return yes if cond is True else no if cond is False else jnp.where(cond, yes, no)

    forwards = functools.partial(forwards_at, C)
    way_on = functools.partial(way_at, C)
    EVEN, ODD, PAIR, LAST, PIECES = 0, hq, hq + 1, hq + 2, hq + 3
    through, _ = arrivals(C, K, hq, parts)

    load_x = pltpu.make_async_copy(x_ref, x_in, local.at[0])
    load_x.start()
    barrier = pltpu.get_barrier_semaphore()
    row_peers = sorted({d % R for d in range(2, half + 1, 2)} | {-d % R for d in range(2, half + 1, 2)})
    for off in row_peers:
        pl.semaphore_signal(barrier, inc=1, device_id={"row": lax.rem(r + off, R)}, device_id_type=MESH_ID)
    pl.semaphore_signal(barrier, inc=1, device_id={"row": partner}, device_id_type=MESH_ID)
    greeted = len(row_peers) + 1
    for hop in range(1, C):
        for sgn in (1, -1):
            cond = among(lambda n: 0 <= n + sgn * hop < C)[1]

            def greet():
                pl.semaphore_signal(barrier, inc=1, device_id={"col": c + sgn * hop}, device_id_type=MESH_ID)
            when(cond, greet)
            greeted += int(cond) if isinstance(cond, bool) else jnp.where(cond, 1, 0)

    small = (
        (rows_ref, row_of), (cols_ref, col_of), (used_ref, counts_ref), (shift_ref, center_ref), (scale_ref, width_ref))
    loads = [pltpu.make_async_copy(src, dst, local.at[3 + i]) for i, (src, dst) in enumerate(small)]
    for copy in loads:
        copy.start()
    fetch = pltpu.make_async_copy(tiles_ref.at[0], tiles, local.at[1])
    fetch.start()

    def way(sgn, d):
        return 2 * (d - 1) + (0 if sgn > 0 else 1)

    def tiles_at(ref, slot):
        return ref.at[pl.ds(slot * pt, pt)]

    def part_at(ref, slot, u):
        return ref.at[pl.ds(slot * pt + u * ptu, ptu)]

    sgns = (1, -1)
    dists = range(1, C)
    final = {}
    for t in range(2):
        for h in range(K):
            for u in range(parts):
                for sgn in sgns:
                    for d in dists:
                        def test(n):
                            on = way_on(t, h, u, n - sgn * d, sgn, d)
                            return on is not None and on[0] == 0
                        final[t, h, u, sgn, d] = among(test)

    def clear():
        for (t, h, u, sgn, d), (_, cond) in final.items():
            if cond is not True and cond is not False:
                def zero():
                    part_at(col_fin[t][h], way(sgn, d), u)[...] = jnp.zeros((ptu, vcs[h], size), jnp.bfloat16)
                pl.when(jnp.logical_not(cond))(zero)
        for t in range(2):
            for h in range(K):
                tiles_at(pair_in[t][h], hq)[...] = jnp.zeros((pt, vcs[h], size), jnp.bfloat16)
        for h in range(K):
            back[h][slots] = jnp.zeros((vcs[h], size), jnp.float32)
            direct[h][slots] = jnp.zeros((vcs[h], size), jnp.float32)

    with SCOPE("loadx"):
        load_x.wait()
    for j in range(pt):
        block = x_in[j * size:(j + 1) * size, :].astype(jnp.float32).T.astype(jnp.bfloat16)
        for h in range(K):
            part = block[begins[h]:begins[h] + vcs[h], :]
            win[0][h][j] = part
            seg[0][h][c * pt + j] = part
    with SCOPE("greet"):
        pl.semaphore_wait(barrier, greeted)

    sends = [0] * C

    def grains(count, h):
        return count * ptu * (vcs[h] // GRAIN)

    def start(copy, h, whom=everyone, count=parts):
        when(whom[1], copy.start)
        for n in whom[0]:
            sends[n] += grains(count, h)

    def to_row(src, dst, t, h, sem, row):
        return pltpu.make_async_remote_copy(
            src_ref=src, dst_ref=dst, send_sem=sent, recv_sem=arrived.at[t, h, sem],
            device_id={"row": row}, device_id_type=MESH_ID)

    def to_col(src, dst, t, h, sem, col):
        return pltpu.make_async_remote_copy(
            src_ref=src, dst_ref=dst, send_sem=sent, recv_sem=arrived.at[t, h, sem],
            device_id={"col": col}, device_id_type=MESH_ID)

    def await_pieces(t, h, sem, count):
        view = spare.at[pl.ds(0, grains(count, h))]
        to_row(view, view, t, h, sem, partner).wait_recv()

    def by_count(counts, act):
        for count in sorted(set(counts) - {0}):
            when(among(lambda n: counts[n] == count)[1], lambda: act(count))

    def up(d):
        return lax.rem(r + d, R)

    def start_row(t, h):
        own = tiles_at(win[t][h], 0)
        for d in range(hq, 0, -1):
            start(to_row(own, tiles_at(win[t][h], 2 * d), t, h, EVEN + d - 1, up(R - 2 * d)), h)
        pl.when(k == 1)(to_row(own, tiles_at(win[t][h], 1), t, h, ODD, partner).start)

    def forward_row(t, h, d):
        await_pieces(t, h, EVEN + d - 1, parts)
        view = tiles_at(win[t][h], 2 * d)
        copy = to_row(view, tiles_at(win[t][h], 2 * d - 1 + 2 * k), t, h, ODD, partner)
        if d < hq:
            start(copy, h)
        else:
            pl.when(k == 0)(copy.start)
            for n in range(C):
                sends[n] += grains(parts, h)

    def col_piece(t, h, u, sgn, d, hop):
        view = part_at(seg[t][h], c - sgn * d, u)
        src = view if d else part_at(win[t][h], 0, u)
        sem = pick(lambda n: forwards(t, h, u, n + sgn * hop, sgn, d + hop),
                   through.get((t, h, u, "gather", sgn, d + hop), 0), PIECES)
        return to_col(src, view, t, h, sem, c + sgn * hop)

    def start_col(t, h, u):
        for hop in reversed(dists):
            for sgn in sgns:
                def test(n):
                    return 0 <= n + sgn * hop < C and parent(GATHER_TREES[t][h][u], side(C - 1 - n, sgn, C), hop) == 0
                whom = among(test)
                if whom[0]:
                    start(col_piece(t, h, u, sgn, 0, hop), h, whom, 1)

    def forward_col(t, h, d, rel, u):
        for sgn in sgns:
            whom = among(lambda n: forwards(t, h, u, n, sgn, d) and is_long(C, n, sgn) == (rel == "L"))
            if whom[0]:
                when(whom[1], lambda: await_pieces(t, h, through[t, h, u, "gather", sgn, d], 1))
                start(col_piece(t, h, u, sgn, d, 1), h, whom, 1)

    def products(source, index_ref, link_row, sums, weights):
        def one(s, carry):
            term = lax.dot_general(
                source[index_ref[0, s]], weights[s], (((1,), (0,)), ((), ())),
                preferred_element_type=jnp.float32)
            sums[s] = sums[links[link_row, s]] + term
            return carry

        lax.fori_loop(0, slots, one, 0, unroll=UNROLL)

    def pass_on(t, h, d, rel, u):
        for sgn in sgns:
            found = sorted({way_on(t, h, u, n, sgn, d) for n in range(C)} - {None})
            for left, helped in found:
                if helped != bool(rel):
                    continue
                whom = among(lambda n: way_on(t, h, u, n, sgn, d) == (left, helped)
                             and (not rel or is_long(C, n, sgn) == (rel == "L")))
                if not whom[0]:
                    continue
                w = way(sgn, d)

                def act():
                    if helped:
                        await_pieces(t, h, through[t, h, u, "reduce", sgn, d], 1)
                    dest = c + sgn * d
                    for j in range(u * ptu, (u + 1) * ptu):
                        value = direct[h][links[2, dest * pt + j]]
                        if helped:
                            value += col_mid[t][h][w * pt + j].astype(jnp.float32)
                        col_out[t][h][w * pt + j] = value.astype(jnp.bfloat16)
                when(whom[1], act)
                src = part_at(col_out[t][h], w, u)
                if left == 0:
                    copy = to_col(src, part_at(col_fin[t][h], w, u), t, h, LAST, c + sgn * d)
                else:
                    copy = to_col(src, part_at(col_mid[t][h], way(sgn, left), u), t, h,
                                  through[t, h, u, "reduce", sgn, left], c + sgn * (d - left))
                start(copy, h, whom, 1)

    def do_direct(t, h):
        await_pieces(t, h, ODD, hq * parts)
        products(win[t][h], col_of, 0, direct[h], flipped)
        for u in range(parts):
            for d in reversed(dists):
                pass_on(t, h, d, "", u)

    def do_back(t, h):
        held = [sum(forwards(t, h, u, n, sgn, d) for u in range(parts) for sgn in sgns for d in dists) for n in range(C)]
        by_count([(C - 1) * parts - held[n] for n in range(C)], lambda count: await_pieces(t, h, PIECES, count))
        products(seg[t][h], row_of, 1, back[h], tiles)
        for i in range(1, hq + 1):
            for j in range(pt):
                pair_out[t][h][(i - 1) * pt + j] = back[h][links[3, (2 * i - 1) * pt + j]].astype(jnp.bfloat16)
            start(to_row(tiles_at(pair_out[t][h], i - 1), tiles_at(pair_in[t][h], i - 1), t, h, PAIR, partner), h)

    def return_row(t, h):
        await_pieces(t, h, PAIR, hq * parts)
        for d in range(hq, 0, -1):
            for j in range(pt):
                value = back[h][links[3, 2 * d * pt + j]] + pair_in[t][h][(d - 1 + k) * pt + j].astype(jnp.float32)
                row_out[t][h][(d - 1) * pt + j] = value.astype(jnp.bfloat16)
            start(to_row(tiles_at(row_out[t][h], d - 1), tiles_at(row_in[t][h], d - 1), t, h, LAST, up(2 * d)), h)


    def finish(t, h):
        ends = [hq * parts + sum(n in final[t, h, u, sgn, d][0] for u in range(parts) for sgn in sgns for d in dists)
                for n in range(C)]
        by_count(ends, lambda count: await_pieces(t, h, LAST, count))
        slot = jnp.where(k == 1, 0, hq)
        for j in range(pt):
            total = back[h][links[3, j]] + direct[h][links[2, c * pt + j]]
            total += pair_in[t][h][slot * pt + j].astype(jnp.float32)
            for d in range(hq):
                total += row_in[t][h][d * pt + j].astype(jnp.float32)
            for sgn in sgns:
                for d in dists:
                    if final[t, h, j // ptu, sgn, d][0]:
                        total += col_fin[t][h][way(sgn, d) * pt + j].astype(jnp.float32)
            begin = win[0][h][j].astype(jnp.float32)
            shift, width = center_ref[0], width_ref[0]
            if t == 0:
                first = ((total - shift * begin) / width).astype(jnp.bfloat16)
                win[1][h][j] = first
                seg[1][h][c * pt + j] = first
            else:
                first = win[1][h][j].astype(jnp.float32)
                result[j, begins[h]:begins[h] + vcs[h], :] = 2.0 * (total - shift * first) / width - begin

    def link_slots():
        for copy in loads:
            copy.wait()
        count = counts_ref[0, 0]
        sub = lax.broadcasted_iota(jnp.int32, (slots, size), 0)
        lane = lax.broadcasted_iota(jnp.int32, (slots, size), 1)
        for i, keys in enumerate((row_of, col_of)):
            key = jnp.full((slots, size), -1, jnp.int32)
            column = key
            for s in range(slots):
                one = keys[0, s]
                key = jnp.where(lane == s, one, key)
                column = jnp.where(sub == s, one, column)
            used = sub < count
            same = (column == key) & (sub < lane) & used
            before = jnp.max(jnp.where(same, sub, -1), axis=0, keepdims=True)
            table[i:i + 1, :] = jnp.where(before < 0, slots, before)
            last = jnp.max(jnp.where((column == lane) & used, sub, -1), axis=0, keepdims=True)
            table[2 + i:3 + i, :] = jnp.where(last < 0, slots, last)
        publish = pltpu.make_async_copy(table, links, local.at[2])
        publish.start()
        fetch.wait()

        def flip(s, carry):
            flipped[s] = tiles[s].astype(jnp.float32).T.astype(jnp.bfloat16)
            return carry

        lax.fori_loop(0, slots, flip, 0, unroll=UNROLL)
        publish.wait()

    acts = {
        "GX": start_row, "GZ": start_col, "XF": forward_row, "GF": forward_col, "D": do_direct, "RM": pass_on,
        "B": do_back, "RX": return_row, "E": finish}
    first = {("GX", 0, 0)} | {("GZ", 0, 0, u) for u in range(parts)}
    for kind, *args in full_order(K, C, hq, parts):
        with SCOPE(kind + "".join(str(a) for a in args)):
            acts[kind](*args)
        if first:
            first.discard((kind, *args))
            if not first:
                with SCOPE("link"):
                    clear()
                    link_slots()
    with SCOPE("out"):
        for j in range(pt):
            out_ref[j * size:(j + 1) * size, :] = result[j].T.astype(jnp.bfloat16)
    with SCOPE("drain"):
        def drained(count):
            view = spare.at[pl.ds(0, count)]
            to_row(view, view, 0, 0, 0, partner).wait_send()
        by_count(sends, drained)


def per_device(start_vectors, tiles, tile_rows, tile_cols, tile_counts, center, half_width):
    R = lax.axis_size("row")
    C = lax.axis_size("col")
    half = R // 2
    hq = half // 2
    piece_rows, vec = start_vectors.shape
    size = tiles.shape[-1]
    slots = tiles.shape[1]
    pt = piece_rows // size
    vcs = widths(vec)
    ways = 2 * (C - 1)
    parts = parts_of(pt)
    nsem = arrivals(C, CHUNKS, hq, parts)[1]
    most = 2 * (4 * hq + 4 * C) * pt * (vec // GRAIN)
    vmem = pl.BlockSpec(memory_space=pltpu.VMEM)
    bf, f32, i32 = jnp.bfloat16, jnp.float32, jnp.int32

    def pair(count):
        return [pltpu.VMEM((count * pt, vc, size), bf) for vc in vcs * 2]

    scratch = (
        pair(half + 1) + pair(C) + pair(hq) + pair(hq) + pair(hq + 1) + pair(hq)
        + pair(ways) + pair(ways) + pair(ways)
        + [pltpu.VMEM((slots + 1, vc, size), f32) for vc in vcs * 2]
        + [
            pltpu.VMEM((piece_rows, vec), bf), pltpu.VMEM((pt, vec, size), f32),
            pltpu.VMEM((slots, size, size), bf), pltpu.VMEM((slots, size, size), bf),
            pltpu.VMEM((most, GRAIN, size), bf),
            pltpu.VMEM((4, size), i32),
            pltpu.SMEM((1, slots), i32), pltpu.SMEM((1, slots), i32),
            pltpu.SMEM((1, 1), i32), pltpu.SMEM((1,), f32), pltpu.SMEM((1,), f32), pltpu.SMEM((4, size), i32),
        ]
        + [pltpu.SemaphoreType.DMA((8,)), pltpu.SemaphoreType.DMA, pltpu.SemaphoreType.DMA((2, CHUNKS, nsem))]
    )
    return pl.pallas_call(
        functools.partial(filter_kernel, (R, C, half, pt, slots, vec, size)),
        out_shape=jax.ShapeDtypeStruct((piece_rows, vec), bf),
        in_specs=[pl.BlockSpec(memory_space=pltpu.HBM)] * 4 + [pl.BlockSpec(memory_space=pl.ANY)] * 3,
        out_specs=vmem,
        scratch_shapes=scratch,
        compiler_params=pltpu.CompilerParams(
            collective_id=0, has_side_effects=True, vmem_limit_bytes=VMEM_LIMIT),
        name="filter_steps",
    )(*[pltpu.with_memory_space_constraint(a, pltpu.HBM) for a in (start_vectors, tiles, tile_rows, tile_cols)],
      tile_counts, center, half_width)


VMEM_LIMIT = 48 << 20


def solution(mesh):
    return jax.shard_map(
        per_device,
        mesh=mesh,
        in_specs=(
            P(("row", "col"), None),
            P("row", "col", None, None),
            P("row", "col"),
            P("row", "col"),
            P("row", "col"),
            P(),
            P(),
        ),
        out_specs=P(("row", "col"), None),
        check_vma=False,
    )
```
